128 devices in a mesh: lat: 4 (over y_hi, core), grp: 32 (over z, x, y_lo).
Axes of the slice: x: 4, y: 4 (y_hi: 2, y_lo: 2; y = y_hi * 2 + y_lo), z: 4, core: 2. Of those that a mesh axis runs over, the one named last changes fastest.
Arguments:
- inputs: bfloat16 [256, 1024, 1024], P(None, ('lat', 'grp')), may hold values from -6 to 6
- w_in: bfloat16 [256, 512], replicated, may hold values from -0.375 to 0.375
- bias_in: float32 [512], replicated, may hold values from -3 to 3
- w_out: bfloat16 [512, 256], replicated, may hold values from -0.25 to 0.25
- advected: bfloat16 [256, 1024, 1024], P('grp', 'lat'), may hold values from -6 to 6
- cotangent: bfloat16 [256, 1024, 1024], P('grp', 'lat'), may hold values from -6 to 6
- offsets: int32 [2, 64, 4], P(None, 'lat'), may hold values from 0 to 3
- stencil_row: int32 [64, 4], P('lat'), may hold values from 0 to 4
- stencil_col: int32 [64, 4], P('lat'), may hold values from 0 to 124
- fracs: float32 [2, 64, 4], P(None, 'lat'), may hold values from 0 to 1
Outputs:
- grad_inputs: bfloat16 [256, 1024, 1024], P(None, ('lat', 'grp'))
- grad_w_in: float32 [256, 512], P(None, ('lat', 'grp'))
- grad_bias: float32 [512], P(('lat', 'grp'))
- grad_w_out: float32 [512, 256], P(('lat', 'grp'))
- grad_frac: float32 [2, 64, 4], P(None, 'lat')
The draws below stay inside these ranges and needn't reach their ends.
All inputs are finite; a program needn't handle non-finite values.
Results may differ from the reference program's by a relative error of at most 0.0068.
Values may be sent and summed in bfloat16 or wider, within the bound.
No kernel may reach another device: no remote copies, remote signals or barrier semaphores. Data moves between devices by JAX's collectives and lax.ppermute only.
A program may use at most 128 MiB of HBM per device.

```python
import jax
import jax.numpy as jnp
from jax import lax

C = 256
HID = 512
WCOL = 1024
BH = 16
BW = 256
NROWS = 1024
RBLK = 64
CBLK = 4


def with_ends(values, own_key, low, largest):
    longest = values.shape.index(max(values.shape))
    spots = []
    for shift in (0, 1):
        where = [jax.random.randint(jax.random.fold_in(own_key, axis), (), 0, length) for axis, length in enumerate(values.shape)]
        where[longest] = (where[longest] + shift) % values.shape[longest]
        spots.append(tuple(where))
    return values.at[spots[0]].set(low).at[spots[1]].set(largest)


def levels(stream_key, dims, cuts, smallest, high):
    level, own = 1.0, jax.random.fold_in(stream_key, 6)
    for dim, parts in cuts:
        steps = jnp.exp(jax.random.uniform(jax.random.fold_in(own, dim), (parts,), jnp.float32, smallest / len(cuts), high / len(cuts)))
        level = level * jnp.repeat(steps, dims[dim] // parts).reshape([-1 if axis == dim else 1 for axis in range(len(dims))])
    return level


def noise(rng, extent, scale, bound, cuts=(), held_as=jnp.bfloat16):
    array = jax.random.normal(rng, extent, jnp.float32) * scale
    if len(cuts) > 0:
        array = levels(rng, extent, cuts, -0.22, 0.18) * array
    return jnp.clip(array, min=-bound, max=bound).astype(held_as)


def setup_inputs(seed: int = 0) -> dict:
    seeds = jax.random.split(jax.random.key(seed), 11)
    return {
        "inputs": noise(seeds[0], (C, NROWS, WCOL), 1.0, 6.0, ((1, 128),)),
        "w_in": noise(seeds[1], (C, HID), C ** -0.5, 0.375),
        "bias_in": noise(seeds[2], (HID,), 0.5, 3.0, (), jnp.float32),
        "w_out": noise(seeds[3], (HID, C), HID ** -0.5, 0.25),
        "advected": noise(seeds[4], (C, NROWS, WCOL), 1.0, 6.0, ((0, 32), (1, 4))),
        "cotangent": noise(seeds[5], (C, NROWS, WCOL), 1.0, 6.0, ((0, 32), (1, 4))),
        "offsets": with_ends(jax.random.randint(seeds[6], (2, RBLK, CBLK), 0, 4), jax.random.fold_in(seeds[6], 1), 0, 3).astype(jnp.int32),
        "stencil_row": with_ends(jax.random.randint(seeds[7], (RBLK, CBLK), 0, BH // 2 - 3), jax.random.fold_in(seeds[7], 1), 0, (BH // 2 - 3) - 1).astype(jnp.int32),
        "stencil_col": with_ends(jax.random.randint(seeds[8], (RBLK, CBLK), 0, BW // 2 - 3), jax.random.fold_in(seeds[8], 1), 0, (BW // 2 - 3) - 1).astype(jnp.int32),
        "fracs": jnp.clip(1.0 * jax.random.uniform(seeds[9], (2, RBLK, CBLK), jnp.float32) ** levels(seeds[9], (2, RBLK, CBLK), ((1, 4),), -0.2, 0.2), 0.0, 1.0),
    }


def catmull(frac):
    square = frac * frac
    cube = square * frac
    weights = (0.5 * (-cube + 2.0 * square - frac), 0.5 * (3.0 * cube - 5.0 * square + 2.0), 0.5 * (-3.0 * cube + 4.0 * square + frac), 0.5 * (cube - square))
    slopes = (0.5 * (-3.0 * square + 4.0 * frac - 1.0), 0.5 * (9.0 * square - 10.0 * frac), 0.5 * (-9.0 * square + 8.0 * frac + 1.0), 0.5 * (3.0 * square - 2.0 * frac))
    return (weights, slopes)

def band_matrix(position, frac, inner):
    offset_grid = jnp.arange(3 * inner, dtype=jnp.int32)[None, None, :] - jnp.arange(inner, dtype=jnp.int32)[None, :, None] - position[:, None, None]
    weights, slopes = catmull(frac)
    value = jnp.zeros(offset_grid.shape, frac.dtype)
    slope = jnp.zeros(offset_grid.shape, frac.dtype)
    for tap in range(4):
        value = value + jnp.where(offset_grid == tap, weights[tap][:, None, None], 0.0)
        slope = slope + jnp.where(offset_grid == tap, slopes[tap][:, None, None], 0.0)
    return (value.astype(jnp.bfloat16), slope.astype(jnp.bfloat16))

def row_pass(drow, window, row_pos, row_frac, col_pos, col_frac):
    channels = drow.shape[0]
    blocks = drow.shape[2] // BW
    ry_value, ry_slope = band_matrix(row_pos, row_frac, BH)
    rx_value, rx_slope = band_matrix(col_pos, col_frac, BW)
    rx_both = jnp.concatenate([rx_value, rx_slope], axis=2).astype(jnp.float32)
    pieces = drow.reshape(channels, BH, blocks, BW).astype(jnp.float32)
    product = jnp.einsum('chbw,bwv->bchv', pieces, rx_both)
    z_value = product[..., :3 * BW]
    z_slope = product[..., 3 * BW:]
    z_round = z_value.astype(jnp.bfloat16).astype(jnp.float32)
    spread = jnp.einsum('bho,bchv->bcov', ry_value.astype(jnp.float32), z_round)
    windows = jnp.stack([window[:, :, column * BW:column * BW + 3 * BW] for column in range(blocks)])
    ry_both = jnp.concatenate([ry_value, ry_slope], axis=1).astype(jnp.float32)
    lifted = jnp.einsum('bjo,bcov->bcjv', ry_both, windows.astype(jnp.float32))
    grad_row = lax.optimization_barrier(jnp.sum(lifted[:, :, BH:] * z_value, axis=(1, 2, 3)))
    grad_col = lax.optimization_barrier(jnp.sum(lifted[:, :, :BH] * z_slope, axis=(1, 2, 3)))
    split = spread.reshape(blocks, channels, 3, BH, 3, BW)
    summed = jnp.roll(split[:, :, :, :, 0, :], -1, axis=0)
    summed = summed + split[:, :, :, :, 1, :]
    summed = summed + jnp.roll(split[:, :, :, :, 2, :], 1, axis=0)
    contrib = summed.transpose(2, 1, 3, 0, 4).reshape(3, channels, BH, blocks * BW)
    return (contrib, jnp.stack([grad_row, grad_col]))

def reference(inputs, w_in, bias_in, w_out, advected, cotangent, offsets, stencil_row, stencil_col, fracs):
    padded = jnp.pad(advected, ((0, 0), (BH, BH), (0, 0)))
    widened = jnp.concatenate([padded[:, :, WCOL - BW:], padded, padded[:, :, :BW]], axis=2)
    row_pos = BH // 2 * offsets[0] + stencil_row
    col_pos = BW // 2 * offsets[1] + stencil_col

    def one_row(index):
        drow = lax.dynamic_slice_in_dim(cotangent, index * BH, BH, 1)
        window = lax.dynamic_slice_in_dim(widened, index * BH, 3 * BH, 1)
        return row_pass(drow, window, row_pos[index], fracs[0][index], col_pos[index], fracs[1][index])
    contribs, frac_terms = lax.map(one_row, jnp.arange(RBLK, dtype=jnp.int32))
    extended = jnp.zeros((RBLK + 2, C, BH, WCOL), contribs.dtype)
    for shift in range(3):
        extended = extended + jnp.pad(contribs[:, shift], ((shift, 2 - shift), (0, 0), (0, 0), (0, 0)))
    dy = extended[1:RBLK + 1].transpose(1, 0, 2, 3).reshape(C, NROWS, WCOL).astype(jnp.bfloat16)
    grad_frac = jnp.transpose(frac_terms, (1, 0, 2)) / jnp.sqrt(jnp.float32(C * BH * BW))

    def mlp_block(carry, index):
        grad_one, grad_two, grad_three = carry
        x_flat = lax.dynamic_slice_in_dim(inputs, index * BH, BH, 1).reshape(C, BH * WCOL)
        dy_flat = lax.dynamic_slice_in_dim(dy, index * BH, BH, 1).reshape(C, BH * WCOL)
        pre_act = jnp.dot(w_in.T, x_flat, preferred_element_type=jnp.float32) + bias_in[:, None]
        sigma = jax.nn.sigmoid(pre_act)
        act = (pre_act * sigma).astype(jnp.bfloat16)
        dact = jnp.dot(w_out, dy_flat, preferred_element_type=jnp.float32)
        dpre = (dact * sigma * (1.0 + pre_act * (1.0 - sigma))).astype(jnp.bfloat16)
        dx_flat = dy_flat.astype(jnp.float32) + jnp.dot(w_in, dpre, preferred_element_type=jnp.float32)
        grad_one = grad_one + jnp.dot(x_flat, dpre.T, preferred_element_type=jnp.float32)
        grad_two = grad_two + lax.optimization_barrier(jnp.sum(dpre.astype(jnp.float32), axis=1))
        grad_three = grad_three + jnp.dot(act, dy_flat.T, preferred_element_type=jnp.float32)
        return ((grad_one, grad_two, grad_three), dx_flat.astype(jnp.bfloat16).reshape(C, BH, WCOL))
    start = (jnp.zeros((C, HID), jnp.float32), jnp.zeros((HID,), jnp.float32), jnp.zeros((HID, C), jnp.float32))
    sums, dx_blocks = lax.scan(mlp_block, start, jnp.arange(NROWS // BH, dtype=jnp.int32))
    grad_inputs = dx_blocks.transpose(1, 0, 2, 3).reshape(C, NROWS, WCOL)
    scale = 1.0 / jnp.sqrt(jnp.float32(NROWS * WCOL))
    return (grad_inputs, sums[0] * scale, sums[1] * scale, sums[2] * scale, grad_frac)
```

```python
import math

import jax
import jax.numpy as jnp
from jax import lax
from jax.experimental import pallas as pl
from jax.experimental.pallas import tpu as pltpu
from jax.sharding import PartitionSpec as P

C = 256
BH = 16
BW = 256
LANES = 128
HID = 512
F32 = jnp.float32
BF16 = jnp.bfloat16


def catmull(frac):
    square = frac * frac
    cube = square * frac
    weights = (
        0.5 * (-cube + 2.0 * square - frac),
        0.5 * (3.0 * cube - 5.0 * square + 2.0),
        0.5 * (-3.0 * cube + 4.0 * square + frac),
        0.5 * (cube - square),
    )
    slopes = (
        0.5 * (-3.0 * square + 4.0 * frac - 1.0),
        0.5 * (9.0 * square - 10.0 * frac),
        0.5 * (-9.0 * square + 8.0 * frac + 1.0),
        0.5 * (3.0 * square - 2.0 * frac),
    )
    return (jnp.stack(weights, axis=-1), jnp.stack(slopes, axis=-1))


def rounded(values):
    return lax.reduce_precision(values, 8, 7)


def halo(band, dim, width):
    count = lax.axis_size("lat")
    size = band.shape[dim]
    head = lax.slice_in_dim(band, 0, width, axis=dim)
    tail = lax.slice_in_dim(band, size - width, size, axis=dim)
    above = lax.ppermute(tail, "lat", [(i, i + 1) for i in range(count - 1)])
    below = lax.ppermute(head, "lat", [(i + 1, i) for i in range(count - 1)])
    return above, below


def diagonal():
    row = lax.broadcasted_iota(jnp.int32, (LANES, 2 * LANES), 0)
    col = lax.broadcasted_iota(jnp.int32, (LANES, 2 * LANES), 1)
    return col - row


def channel_minor():
    out = lax.broadcasted_iota(jnp.int32, (LANES, LANES), 0)
    src = lax.broadcasted_iota(jnp.int32, (LANES, LANES), 1)
    return ((out % 8) * 16 + out // 8 == src).astype(F32).astype(BF16)


def taps(masks, weights):
    value = jnp.zeros((LANES, 2 * LANES), F32)
    for tap in range(4):
        value = jnp.where(masks[tap], weights[tap], value)
    return value.astype(BF16)


def spread_body(pos_ref, wgt_ref, top_ref, mid_ref, bot_ref, out_ref, row_scr, cot_scr, z_scr, acc):
    step = pl.program_id(0)
    last = pl.num_programs(0) - 1

    @pl.when(step == 0)
    def _():
        acc[0 : 2 * BH] = jnp.zeros((2 * BH,) + acc.shape[1:], F32)
        row_scr[...] = top_ref[...]

    @pl.when(step == last)
    def _():
        row_scr[...] = bot_ref[...]

    @pl.when(jnp.logical_and(step > 0, step < last))
    def _():
        row_scr[...] = mid_ref[...]

    acc[pl.ds((step + 2) * BH, BH)] = jnp.zeros((BH,) + acc.shape[1:], F32)
    rows = row_scr[...].reshape(LANES, row_scr.shape[2])
    cot_scr[...] = jnp.dot(channel_minor(), rows, preferred_element_type=F32).astype(BF16)
    diag = diagonal()
    for block in range(4):
        base = step * 4 + block
        py = pos_ref[base * 3]
        tile = pos_ref[base * 3 + 1]
        shift = diag - pos_ref[base * 3 + 2]
        masks = [shift == tap for tap in range(4)]
        cols = taps(masks, [wgt_ref[base * 16 + tap] for tap in range(4)])
        wy = [wgt_ref[base * 16 + 4 + tap] for tap in range(4)]
        halves = jnp.concatenate(
            [
                cot_scr[:, block * BW : block * BW + LANES],
                cot_scr[:, block * BW + LANES : (block + 1) * BW],
            ],
            axis=0,
        )
        z_scr[block] = jnp.dot(halves, cols, preferred_element_type=F32)
        for part in range(3):
            if part == 0:
                z = z_scr[block, 0:LANES, 0:LANES]
            elif part == 1:
                z = z_scr[block, 0:LANES, LANES:] + z_scr[block, LANES:, 0:LANES]
            else:
                z = z_scr[block, LANES:, LANES:]
            z = z.astype(BF16).astype(F32).reshape(BH, 8, LANES)
            target = (2 * block + 6 + part + tile) & 7
            for j in range(BH + 3):
                value = None
                for tap in range(4):
                    if 0 <= j - tap < BH:
                        term = wy[tap] * z[j - tap]
                        value = term if value is None else value + term
                at = step * BH + py + j
                acc[at, target] = acc[at, target] + value

    for tile_index in range(8):
        done = acc[pl.ds(step * BH, BH), tile_index].reshape(BH * 8, LANES)
        out_ref[0, :, tile_index * LANES : (tile_index + 1) * LANES] = done.astype(BF16)


def spread(pos, wgt, top, cot, bottom):
    channels, band_rows, columns = cot.shape
    blocks = band_rows // BH
    spec = lambda shape, index: pl.BlockSpec(shape, index)
    return pl.pallas_call(
        spread_body,
        name="spread",
        out_shape=jax.ShapeDtypeStruct((blocks, BH * channels, columns), BF16),
        grid_spec=pltpu.PrefetchScalarGridSpec(
            num_scalar_prefetch=2,
            grid=(blocks + 2,),
            in_specs=[
                spec((channels, BH, columns), lambda g, a, b: (0, 0, 0)),
                spec(
                    (channels, BH, columns),
                    lambda g, a, b: (0, jnp.clip(g - 1, 0, blocks - 1), 0),
                ),
                spec((channels, BH, columns), lambda g, a, b: (0, 0, 0)),
            ],
            out_specs=spec(
                (1, BH * channels, columns), lambda g, a, b: (jnp.maximum(g - 2, 0), 0, 0)
            ),
            scratch_shapes=[
                pltpu.VMEM((channels, BH, columns), BF16),
                pltpu.VMEM((BH * channels, columns), BF16),
                pltpu.VMEM((4, 2 * LANES, 2 * LANES), F32),
                pltpu.VMEM(((blocks + 4) * BH, columns // LANES, channels, LANES), F32),
            ],
        ),
        compiler_params=pltpu.CompilerParams(dimension_semantics=("arbitrary",)),
    )(pos, wgt, top, cot, bottom)


def frac_body(
    pos_ref, wgt_ref, top_ref, mid_ref, next_ref, bot_ref, cot_ref, out_ref, cot_scr, z_scr, field
):
    step = pl.program_id(0)
    last = pl.num_programs(0) - 1
    width = cot_scr.shape[1]
    order = channel_minor()

    def put(row_block, source):
        rows = source[...].reshape(LANES, width)
        moved = jnp.dot(order, rows, preferred_element_type=F32)
        for tile_index in range(8):
            field[pl.ds(row_block * BH, BH), tile_index] = moved[
                :, tile_index * LANES : (tile_index + 1) * LANES
            ].reshape(BH, 8, LANES)

    @pl.when(step == 0)
    def _():
        put(0, top_ref)
        put(1, mid_ref)

    @pl.when(step == last)
    def _():
        put(step + 2, bot_ref)

    @pl.when(step < last)
    def _():
        put(step + 2, next_ref)

    rows = cot_ref[...].reshape(LANES, width)
    cot_scr[...] = jnp.dot(order, rows, preferred_element_type=F32).astype(BF16)
    diag = diagonal()
    for block in range(4):
        base = (step + 1) * 4 + block
        py = pos_ref[base * 3]
        tile = pos_ref[base * 3 + 1]
        shift = diag - pos_ref[base * 3 + 2]
        masks = [shift == tap for tap in range(4)]
        both = jnp.concatenate(
            [
                taps(masks, [wgt_ref[base * 16 + tap] for tap in range(4)]),
                taps(masks, [wgt_ref[base * 16 + 8 + tap] for tap in range(4)]),
            ],
            axis=1,
        )
        halves = jnp.concatenate(
            [
                cot_scr[:, block * BW : block * BW + LANES],
                cot_scr[:, block * BW + LANES : (block + 1) * BW],
            ],
            axis=0,
        )
        z_scr[block] = jnp.dot(halves, both, preferred_element_type=F32)
        by_value = [jnp.zeros((8, LANES), F32) for tap in range(4)]
        by_slope = [jnp.zeros((8, LANES), F32) for tap in range(4)]
        for part in range(3):
            pair = []
            for lane in (0, 2 * LANES):
                if part == 0:
                    z = z_scr[block, 0:LANES, lane : lane + LANES]
                elif part == 1:
                    z = (
                        z_scr[block, 0:LANES, lane + LANES : lane + 2 * LANES]
                        + z_scr[block, LANES:, lane : lane + LANES]
                    )
                else:
                    z = z_scr[block, LANES:, lane + LANES : lane + 2 * LANES]
                pair.append(z.reshape(BH, 8, LANES))
            source = (2 * block + 6 + part + tile) & 7
            for j in range(BH + 3):
                value = field[step * BH + py + j, source]
                for tap in range(4):
                    if 0 <= j - tap < BH:
                        by_value[tap] = by_value[tap] + value * pair[0][j - tap]
                        by_slope[tap] = by_slope[tap] + value * pair[1][j - tap]
        first = jnp.zeros((8, LANES), F32)
        second = jnp.zeros((8, LANES), F32)
        for tap in range(4):
            first = first + wgt_ref[base * 16 + 12 + tap] * by_value[tap]
            second = second + wgt_ref[base * 16 + 4 + tap] * by_slope[tap]
        out_ref[0, block] = first
        out_ref[1, block] = second


def frac_sums(pos, wgt, top, field, bottom, cot):
    channels, band_rows, columns = cot.shape
    blocks = band_rows // BH
    shape = (channels, BH, columns)
    return pl.pallas_call(
        frac_body,
        name="frac_sums",
        out_shape=jax.ShapeDtypeStruct((2, blocks * 4, 8, LANES), F32),
        grid_spec=pltpu.PrefetchScalarGridSpec(
            num_scalar_prefetch=2,
            grid=(blocks,),
            in_specs=[
                pl.BlockSpec(shape, lambda g, a, b: (0, 0, 0)),
                pl.BlockSpec(shape, lambda g, a, b: (0, 0, 0)),
                pl.BlockSpec(shape, lambda g, a, b: (0, jnp.minimum(g + 1, blocks - 1), 0)),
                pl.BlockSpec(shape, lambda g, a, b: (0, 0, 0)),
                pl.BlockSpec(shape, lambda g, a, b: (0, g, 0)),
            ],
            out_specs=pl.BlockSpec((2, 4, 8, LANES), lambda g, a, b: (0, g, 0, 0)),
            scratch_shapes=[
                pltpu.VMEM((BH * channels, columns), BF16),
                pltpu.VMEM((4, 2 * LANES, 4 * LANES), F32),
                pltpu.VMEM(((blocks + 2) * BH, columns // LANES, channels, LANES), F32),
            ],
        ),
        compiler_params=pltpu.CompilerParams(dimension_semantics=("arbitrary",)),
    )(pos, wgt, top, field, field, bottom, cot)


def mlp_body(x_ref, dy_ref, w_in_t, w_in, w_out, bias, dx_ref, g_in, g_out, g_bias, dy_scr):
    @pl.when(jnp.logical_and(pl.program_id(0) == 0, pl.program_id(1) == 0))
    def _():
        g_in[...] = jnp.zeros_like(g_in)
        g_out[...] = jnp.zeros_like(g_out)
        g_bias[...] = jnp.zeros_like(g_bias)

    width = x_ref.shape[2]
    dy_scr[...] = dy_ref[...].reshape(C, width)
    x = x_ref[0]
    dy = dy_scr[...]
    pre = jnp.dot(w_in_t[...], x, preferred_element_type=F32) + bias[...]
    sigma = 0.5 + 0.5 * jnp.tanh(0.5 * pre)
    act = (pre * sigma).astype(BF16)
    dact = jnp.dot(w_out[...], dy, preferred_element_type=F32)
    dpre = (dact * sigma * (1.0 + pre * (1.0 - sigma))).astype(BF16)
    dx = dy.astype(F32) + jnp.dot(w_in[...], dpre, preferred_element_type=F32)
    dx_ref[0] = dx.astype(BF16)
    points = (((1,), (1,)), ((), ()))
    g_in[...] += lax.dot_general(dpre, x, points, preferred_element_type=F32)
    g_out[...] += lax.dot_general(act, dy, points, preferred_element_type=F32)
    total = g_bias[...]
    for lane in range(0, width, LANES):
        total = total + dpre[:, lane : lane + LANES].astype(F32)
    g_bias[...] = total


def mlp(x, dy, w_in, bias, w_out):
    rows, channels, columns = x.shape
    sources = dy.shape[0]
    width = 512
    whole = lambda shape: pl.BlockSpec(shape, lambda r, c: (0, 0))
    return pl.pallas_call(
        mlp_body,
        name="mlp",
        out_shape=(
            jax.ShapeDtypeStruct((rows, channels, columns), BF16),
            jax.ShapeDtypeStruct((HID, channels), F32),
            jax.ShapeDtypeStruct((HID, channels), F32),
            jax.ShapeDtypeStruct((HID, LANES), F32),
        ),
        grid=(rows, columns // width),
        in_specs=[
            pl.BlockSpec((1, channels, width), lambda r, c: (r, 0, c)),
            pl.BlockSpec((sources, None, 8, width), lambda r, c: (0, r, 0, c)),
            whole((HID, channels)),
            whole((channels, HID)),
            whole((HID, channels)),
            whole((HID, 1)),
        ],
        out_specs=[
            pl.BlockSpec((1, channels, width), lambda r, c: (r, 0, c)),
            whole((HID, channels)),
            whole((HID, channels)),
            whole((HID, LANES)),
        ],
        scratch_shapes=[pltpu.VMEM((channels, width), BF16)],
        compiler_params=pltpu.CompilerParams(dimension_semantics=("arbitrary", "arbitrary")),
    )(x, dy, w_in.T, w_in, w_out, bias[:, None])


def shards(
    inputs, w_in, bias_in, w_out, advected, cotangent, offsets, stencil_row, stencil_col, fracs
):
    channels_dev, band_rows, columns = advected.shape
    row_blocks = band_rows // BH
    point_rows = inputs.shape[1]
    lat = lax.axis_size("lat")
    grp = lax.axis_size("grp")

    cot_top, cot_bottom = halo(cotangent, 1, BH)
    meta = jnp.concatenate(
        [
            offsets.astype(F32),
            stencil_row.astype(F32)[None],
            stencil_col.astype(F32)[None],
            fracs,
        ],
        axis=0,
    )
    meta_top, meta_bottom = halo(meta, 1, 1)
    adv_top, adv_bottom = halo(advected, 1, BH)
    meta = jnp.concatenate([meta_top, meta, meta_bottom], axis=1)
    row_pos = BH // 2 * meta[0] + meta[2]
    pos = jnp.stack([row_pos, meta[1], meta[3]], axis=-1).astype(jnp.int32).reshape(-1)
    row_w, row_s = catmull(meta[4])
    col_w, col_s = catmull(meta[5])
    wgt = rounded(jnp.concatenate([col_w, row_w, col_s, row_s], axis=-1)).reshape(-1)

    dy_band = spread(pos, wgt, cot_top, cotangent, cot_bottom)
    dy_send = dy_band.reshape(grp, point_rows, channels_dev, columns)
    dy_points = lax.all_to_all(dy_send, "grp", split_axis=0, concat_axis=0, tiled=True)
    frac_parts = frac_sums(pos, wgt, adv_top, advected, adv_bottom, cotangent)
    frac_local = jnp.sum(frac_parts, axis=(2, 3)).reshape(-1)

    x_rows = inputs.transpose(1, 0, 2)
    dx_rows, g_in, g_out, g_bias = mlp(x_rows, dy_points, w_in, bias_in, w_out)
    grad_inputs = dx_rows.transpose(1, 0, 2)

    parts = lat * grp
    each = HID // parts
    mine = lax.axis_index("lat")
    slots = jnp.where(jnp.arange(lat) == mine, 1.0, 0.0)[:, None] * frac_local[None]
    slots = jnp.broadcast_to(slots[:, None], (lat, grp, frac_local.shape[0]))
    send = jnp.concatenate(
        [
            g_in.reshape(parts, each * C),
            g_out.reshape(parts, each * C),
            jnp.sum(g_bias, axis=1).reshape(parts, each),
            slots.reshape(parts, -1),
        ],
        axis=1,
    )
    got = lax.all_to_all(send, ("lat", "grp"), split_axis=0, concat_axis=0, tiled=True)
    total = jnp.sum(got, axis=0)
    scale = 1.0 / math.sqrt(point_rows * columns * parts)
    cut = each * C
    grad_first = total[:cut].reshape(each, C).T * scale
    grad_second = total[cut : 2 * cut].reshape(each, C) * scale
    grad_shift = total[2 * cut : 2 * cut + each] * scale
    grad_frac = total[2 * cut + each :].reshape(2, row_blocks, columns // BW)
    grad_frac = grad_frac / math.sqrt(C * BH * BW)
    return (grad_inputs, grad_first, grad_shift, grad_second, grad_frac)


def solution(mesh):
    placed = (
        P(None, ("lat", "grp"), None),
        P(),
        P(),
        P(),
        P("grp", "lat", None),
        P("grp", "lat", None),
        P(None, "lat", None),
        P("lat", None),
        P("lat", None),
        P(None, "lat", None),
    )
    return jax.shard_map(
        shards,
        mesh=mesh,
        in_specs=placed,
        out_specs=(
            P(None, ("lat", "grp"), None),
            P(None, ("lat", "grp")),
            P(("lat", "grp")),
            P(("lat", "grp"), None),
            P(None, "lat", None),
        ),
        check_vma=False,
    )
```

```python
import math

import jax
import jax.numpy as jnp
import numpy as np
from jax import lax
from jax.experimental import pallas as pl
from jax.experimental.pallas import tpu as pltpu
from jax.sharding import PartitionSpec as P

C = 256
BH = 16
BW = 256
LANES = 128
HID = 512
F32 = jnp.float32
BF16 = jnp.bfloat16


CUBIC = (
    (-1.0, 2.0, -1.0, 0.0),
    (3.0, -5.0, 0.0, 2.0),
    (-3.0, 4.0, 1.0, 0.0),
    (1.0, -1.0, 0.0, 0.0),
    (0.0, -3.0, 4.0, -1.0),
    (0.0, 9.0, -10.0, 0.0),
    (0.0, -9.0, 8.0, 1.0),
    (0.0, 3.0, -2.0, 0.0),
)
COL_W, ROW_W, COL_S, ROW_S = 0, 4, 8, 12
EDGE = 11


def catmull(row_frac, col_frac):
    order = (0, 1, 2, 3, 0, 1, 2, 3, 4, 5, 6, 7, 4, 5, 6, 7)
    table = np.asarray([CUBIC[k] for k in order], np.float32)[:, :, None, None]
    on_col = np.asarray([1, 1, 1, 1, 0, 0, 0, 0] * 2, np.bool_)[:, None, None]
    frac = jnp.where(on_col, col_frac[None], row_frac[None])
    square = frac * frac
    cube = square * frac
    value = table[:, 0] * cube + table[:, 1] * square + table[:, 2] * frac + table[:, 3]
    return lax.reduce_precision(0.5 * value, 8, 7)


def exchange(head, tail):
    count = lax.axis_size("lat")
    above = lax.ppermute(tail, "lat", [(i, i + 1) for i in range(count - 1)])
    below = lax.ppermute(head, "lat", [(i + 1, i) for i in range(count - 1)])
    return above, below


def channel_minor():
    out = lax.broadcasted_iota(jnp.int32, (LANES, LANES), 0)
    src = lax.broadcasted_iota(jnp.int32, (LANES, LANES), 1)
    return ((out % 8) * 16 + out // 8 == src).astype(F32).astype(BF16)


def lanes():
    lane = lax.broadcasted_iota(jnp.int32, (8, LANES), 1)
    return lane, lax.broadcasted_iota(jnp.int32, (8, LANES), 0)


def col_taps(weights, shift):
    lane, row = lanes()
    base = jnp.zeros((8, LANES), F32)
    for tap in range(4):
        base = jnp.where(lane - row == tap, weights[tap], base)
    left, right = [], []
    for group in range(0, LANES, 8):
        moved = pltpu.roll(base, (shift + group) & (LANES - 1), 1)
        inside = lane - row >= shift + group
        left.append(jnp.where(inside, moved, 0.0))
        right.append(jnp.where(inside, 0.0, moved))
    both = [jnp.concatenate(left, axis=0), jnp.concatenate(right, axis=0)]
    return jnp.concatenate(both, axis=1).astype(BF16)


REACH = BH + 4


def row_taps(weights):
    lane, row = lanes()
    base = jnp.zeros((8, LANES), F32)
    for tap in range(4):
        base = jnp.where((lane - BH * row + tap) & (LANES - 1) == 0, weights[tap], base)
    own = lane // BH == row
    moved = [base] + [pltpu.roll(base, step, 1) for step in range(1, REACH)]
    return jnp.concatenate([jnp.where(own, part, 0.0) for part in moved], axis=0).astype(BF16)


def pack_body(offs, srow, scol, wgt, *refs):
    sources, (head_ref, tail_ref) = refs[:4], refs[4:]
    channels = sources[0].shape[0]
    last = offs.shape[2] - 1
    lane = lax.broadcasted_iota(jnp.int32, (BH, LANES), 1)
    for side, (out_ref, row) in enumerate(((head_ref, 0), (tail_ref, last))):
        out_ref[0:channels] = sources[2 * side][...]
        out_ref[channels : 2 * channels] = sources[2 * side + 1][...]
        value = jnp.zeros((BH, LANES), F32)
        for block in range(4):
            own = [
                (BH // 2 * offs[0, block, row] + srow[block, row]).astype(F32),
                offs[1, block, row].astype(F32),
                scol[block, row].astype(F32),
            ]
            own = own + [wgt[tap, block, row] for tap in range(8)]
            for slot, entry in enumerate(own):
                value = jnp.where(lane == block * EDGE + slot, entry, value)
        out_ref[2 * channels] = jnp.zeros(out_ref.shape[1:], BF16)
        out_ref[2 * channels, :, 0:LANES] = value.astype(BF16)


def pack(places, cot, adv):
    channels, band_rows, columns = cot.shape
    shape = (2 * channels + 1, BH, columns)
    first = pl.BlockSpec((channels, BH, columns), lambda g, *a: (0, 0, 0))
    last = pl.BlockSpec((channels, BH, columns), lambda g, *a: (0, band_rows // BH - 1, 0))
    return pl.pallas_call(
        pack_body,
        name="pack",
        out_shape=(jax.ShapeDtypeStruct(shape, BF16),) * 2,
        grid_spec=pltpu.PrefetchScalarGridSpec(
            num_scalar_prefetch=4,
            grid=(1,),
            in_specs=[first, first, last, last],
            out_specs=[pl.BlockSpec(shape, lambda g, *a: (0, 0, 0))] * 2,
        ),
        compiler_params=pltpu.CompilerParams(dimension_semantics=("arbitrary",)),
    )(*places, cot, adv, cot, adv)


def spread_blocks(jobs, tap_scr, row_scr, z_scr, acc):
    for job, (rows, block, first, py, tile, shift, wx, wy) in enumerate(jobs):
        tap_scr[job] = col_taps(wx, shift)
        row_scr[job] = row_taps(wy)
    for job, (rows, block, first, py, tile, shift, wx, wy) in enumerate(jobs):
        z = jnp.dot(halves_of(rows, block), tap_scr[job], preferred_element_type=F32)
        z_scr[job, :, 0:LANES] = z[0:LANES, 0:LANES].astype(BF16)
        middle = z[0:LANES, LANES:] + z[LANES:, 0:LANES]
        z_scr[job, :, LANES : 2 * LANES] = middle.astype(BF16)
        z_scr[job, :, 2 * LANES :] = z[LANES:, LANES:].astype(BF16)
    moved = [
        jnp.dot(row_scr[job], z_scr[job], preferred_element_type=F32) for job in range(len(jobs))
    ]
    for job, (rows, block, first, py, tile, shift, wx, wy) in enumerate(jobs):
        for part in range(3):
            target = (2 * block + 6 + part + tile) & 7
            value = moved[job][:, part * LANES : (part + 1) * LANES].reshape(REACH, 8, LANES)
            at = pl.ds(first + py, REACH)
            acc[at, target] = acc[at, target] + value


def spread_scratch():
    return [
        pltpu.VMEM((8, LANES, 2 * LANES), BF16),
        pltpu.VMEM((8, REACH * 8, LANES), BF16),
        pltpu.VMEM((8, LANES, 3 * LANES), BF16),
    ]


def halves_of(rows, block):
    return jnp.concatenate(
        [
            rows[:, block * BW : block * BW + LANES],
            rows[:, block * BW + LANES : (block + 1) * BW],
        ],
        axis=0,
    )


def emit(acc, first, out_ref):
    for tile_index in range(8):
        done = acc[pl.ds(first, BH), tile_index].reshape(BH * 8, LANES)
        out_ref[:, tile_index * LANES : (tile_index + 1) * LANES] = done.astype(BF16)


def spread_body(offs, srow, scol, wgt, cot_ref, out_ref, edge_ref, tap_scr, row_scr, z_scr, acc):
    step = pl.program_id(0)
    last = pl.num_programs(0) - 1

    @pl.when(step == 0)
    def _():
        acc[0 : 2 * BH] = jnp.zeros((2 * BH,) + acc.shape[1:], F32)

    @pl.when(step < last)
    def _():
        acc[pl.ds((2 * step + 2) * BH, 2 * BH)] = jnp.zeros((2 * BH,) + acc.shape[1:], F32)
        jobs = []
        for half in range(2):
            row = 2 * step + half
            rows = cot_ref[:, half * BH : (half + 1) * BH].reshape(LANES, cot_ref.shape[2])
            for block in range(4):
                jobs.append(
                    (
                        rows,
                        block,
                        row * BH,
                        BH // 2 * offs[0, block, row] + srow[block, row],
                        offs[1, block, row],
                        scol[block, row],
                        [wgt[COL_W + tap, block, row] for tap in range(4)],
                        [wgt[ROW_W + tap, block, row] for tap in range(4)],
                    )
                )
        spread_blocks(jobs, tap_scr, row_scr, z_scr, acc)

    emit(acc, jnp.maximum(2 * step - 1, 0) * BH, out_ref.at[0])
    emit(acc, 2 * step * BH, out_ref.at[1])

    @pl.when(step == 0)
    def _():
        edge_ref[0] = acc[BH : 2 * BH]

    @pl.when(step == last)
    def _():
        edge_ref[0] = acc[pl.ds(2 * last * BH, BH)]


def spread(places, cot):
    channels, band_rows, columns = cot.shape
    blocks = band_rows // BH
    pairs = blocks // 2
    tiles = columns // LANES
    return pl.pallas_call(
        spread_body,
        name="spread",
        out_shape=(
            jax.ShapeDtypeStruct((blocks, BH * channels, columns), BF16),
            jax.ShapeDtypeStruct((2, BH, tiles, channels, LANES), F32),
        ),
        grid_spec=pltpu.PrefetchScalarGridSpec(
            num_scalar_prefetch=4,
            grid=(pairs + 1,),
            in_specs=[
                pl.BlockSpec(
                    (channels, 2 * BH, columns), lambda g, *a: (0, jnp.minimum(g, pairs - 1), 0)
                )
            ],
            out_specs=[
                pl.BlockSpec(
                    (2, BH * channels, columns), lambda g, *a: (jnp.maximum(g - 1, 0), 0, 0)
                ),
                pl.BlockSpec(
                    (1, BH, tiles, channels, LANES),
                    lambda g, *a: (jnp.where(g == pairs, 1, 0), 0, 0, 0, 0),
                ),
            ],
            scratch_shapes=spread_scratch()
            + [pltpu.VMEM(((blocks + 2) * BH, tiles, channels, LANES), F32)],
        ),
        compiler_params=pltpu.CompilerParams(dimension_semantics=("arbitrary",)),
    )(*places, cot)


def edge_body(meta, top_ref, bot_ref, edge_ref, whole, out_ref, tap_scr, row_scr, z_scr, acc):
    step = pl.program_id(0)
    upper, lower = 2 * BH, 3 * BH

    @pl.when(step == 0)
    def _():
        acc[0:upper] = jnp.zeros((upper,) + acc.shape[1:], F32)
        acc[upper : upper + BH] = edge_ref[0]
        acc[lower : lower + BH] = edge_ref[1]
        acc[lower + BH :] = jnp.zeros((2 * BH,) + acc.shape[1:], F32)
        jobs = []
        for side, ref in enumerate((top_ref, bot_ref)):
            rows = ref[...].reshape(LANES, ref.shape[2])
            for block in range(4):
                own = [meta[side, block * EDGE + slot] for slot in range(EDGE)]
                place = [entry.astype(jnp.int32) for entry in own[:3]]
                jobs.append((rows, block, side * lower, *place, own[3:7], own[7:11]))
        spread_blocks(jobs, tap_scr, row_scr, z_scr, acc)

    emit(acc, upper + step * BH, out_ref.at[0])


def spread_edges(meta, top, bottom, edges, dy):
    blocks, rows, columns = dy.shape
    channels = edges.shape[3]
    return pl.pallas_call(
        edge_body,
        name="spread_edges",
        out_shape=jax.ShapeDtypeStruct(dy.shape, dy.dtype),
        grid_spec=pltpu.PrefetchScalarGridSpec(
            num_scalar_prefetch=1,
            grid=(2,),
            in_specs=[
                pl.BlockSpec((channels, BH, columns), lambda g, a: (0, 0, 0)),
                pl.BlockSpec((channels, BH, columns), lambda g, a: (0, 0, 0)),
                pl.BlockSpec(edges.shape, lambda g, a: (0, 0, 0, 0, 0)),
                pl.BlockSpec(memory_space=pl.ANY),
            ],
            out_specs=pl.BlockSpec((1, rows, columns), lambda g, a: (g * (blocks - 1), 0, 0)),
            scratch_shapes=spread_scratch() + [pltpu.VMEM((6 * BH,) + edges.shape[2:], F32)],
        ),
        input_output_aliases={4: 0},
        compiler_params=pltpu.CompilerParams(dimension_semantics=("arbitrary",)),
    )(meta, top, bottom, edges, dy)


def frac_body(
    offs, srow, scol, wgt, top_ref, mid_ref, next_ref, bot_ref, cot_ref, out_ref, cot_scr, z_scr, field
):
    step = pl.program_id(0)
    last = pl.num_programs(0) - 1
    width = cot_scr.shape[1]
    order = channel_minor()

    def put(row_block, source):
        rows = source[...].reshape(LANES, width)
        moved = jnp.dot(order, rows, preferred_element_type=F32)
        for tile_index in range(8):
            field[pl.ds(row_block * BH, BH), tile_index] = moved[
                :, tile_index * LANES : (tile_index + 1) * LANES
            ].reshape(BH, 8, LANES)

    @pl.when(step == 0)
    def _():
        put(0, top_ref)
        put(1, mid_ref)

    @pl.when(step == last)
    def _():
        put(step + 2, bot_ref)

    @pl.when(step < last)
    def _():
        put(step + 2, next_ref)

    rows = cot_ref[...].reshape(LANES, width)
    cot_scr[...] = jnp.dot(order, rows, preferred_element_type=F32).astype(BF16)
    for block in range(4):
        py = BH // 2 * offs[0, block, step] + srow[block, step]
        tile = offs[1, block, step]
        shift = scol[block, step]
        both = jnp.concatenate(
            [
                col_taps([wgt[COL_W + tap, block, step] for tap in range(4)], shift),
                col_taps([wgt[COL_S + tap, block, step] for tap in range(4)], shift),
            ],
            axis=1,
        )
        halves = jnp.concatenate(
            [
                cot_scr[:, block * BW : block * BW + LANES],
                cot_scr[:, block * BW + LANES : (block + 1) * BW],
            ],
            axis=0,
        )
        z_scr[block] = jnp.dot(halves, both, preferred_element_type=F32)
        by_value = [jnp.zeros((8, LANES), F32) for tap in range(4)]
        by_slope = [jnp.zeros((8, LANES), F32) for tap in range(4)]
        for part in range(3):
            pair = []
            for lane in (0, 2 * LANES):
                if part == 0:
                    z = z_scr[block, 0:LANES, lane : lane + LANES]
                elif part == 1:
                    z = (
                        z_scr[block, 0:LANES, lane + LANES : lane + 2 * LANES]
                        + z_scr[block, LANES:, lane : lane + LANES]
                    )
                else:
                    z = z_scr[block, LANES:, lane + LANES : lane + 2 * LANES]
                pair.append(z.reshape(BH, 8, LANES))
            source = (2 * block + 6 + part + tile) & 7
            for j in range(BH + 3):
                value = field[step * BH + py + j, source]
                for tap in range(4):
                    if 0 <= j - tap < BH:
                        by_value[tap] = by_value[tap] + value * pair[0][j - tap]
                        by_slope[tap] = by_slope[tap] + value * pair[1][j - tap]
        first = jnp.zeros((8, LANES), F32)
        second = jnp.zeros((8, LANES), F32)
        for tap in range(4):
            first = first + wgt[ROW_S + tap, block, step] * by_value[tap]
            second = second + wgt[ROW_W + tap, block, step] * by_slope[tap]
        out_ref[0, block] = first
        out_ref[1, block] = second


def frac_sums(places, top, field, bottom, cot):
    channels, band_rows, columns = cot.shape
    blocks = band_rows // BH
    shape = (channels, BH, columns)
    return pl.pallas_call(
        frac_body,
        name="frac_sums",
        out_shape=jax.ShapeDtypeStruct((2, blocks * 4, 8, LANES), F32),
        grid_spec=pltpu.PrefetchScalarGridSpec(
            num_scalar_prefetch=4,
            grid=(blocks,),
            in_specs=[
                pl.BlockSpec(shape, lambda g, *a: (1, 0, 0)),
                pl.BlockSpec(shape, lambda g, *a: (0, 0, 0)),
                pl.BlockSpec(shape, lambda g, *a: (0, jnp.minimum(g + 1, blocks - 1), 0)),
                pl.BlockSpec(shape, lambda g, *a: (1, 0, 0)),
                pl.BlockSpec(shape, lambda g, *a: (0, g, 0)),
            ],
            out_specs=pl.BlockSpec((2, 4, 8, LANES), lambda g, *a: (0, g, 0, 0)),
            scratch_shapes=[
                pltpu.VMEM((BH * channels, columns), BF16),
                pltpu.VMEM((4, 2 * LANES, 4 * LANES), F32),
                pltpu.VMEM(((blocks + 2) * BH, columns // LANES, channels, LANES), F32),
            ],
        ),
        compiler_params=pltpu.CompilerParams(dimension_semantics=("arbitrary",)),
    )(*places, top, field, field, bottom, cot)


def mlp_body(
    x_ref, dy_ref, w_in_t, w_in, w_out, half_bias, tail_ref, dx_ref, send_ref, g_in, g_out, g_bias,
    act_scr, dpre_scr
):
    row = pl.program_id(0)

    @pl.when(row == 0)
    def _():
        g_in[...] = jnp.zeros_like(g_in)
        g_out[...] = jnp.zeros_like(g_out)
        g_bias[...] = jnp.zeros_like(g_bias)

    part = 256
    points = (((1,), (1,)), ((), ()))

    def gates(at):
        x = x_ref[0, :, at : at + part]
        dy = dy_ref[:, :, at : at + part].reshape(C, part)
        half = jnp.dot(w_in_t[...], x, preferred_element_type=F32) + half_bias[...]
        twice = 1.0 + jnp.tanh(half)
        act = half * twice
        dact = jnp.dot(w_out[...], dy, preferred_element_type=F32)
        dpre = (dact * (twice + act * (2.0 - twice))).astype(BF16)
        act_scr[:, at : at + part] = act.astype(BF16)
        dpre_scr[:, at : at + part] = dpre
        total = g_bias[...]
        for lane in range(0, part, LANES):
            total = total + dpre[:, lane : lane + LANES].astype(F32)
        g_bias[...] = total

    def products(at):
        x = x_ref[0, :, at : at + part]
        dy = dy_ref[:, :, at : at + part].reshape(C, part)
        dpre = dpre_scr[:, at : at + part]
        dx = dy.astype(F32) + jnp.dot(w_in[...], dpre, preferred_element_type=F32)
        dx_ref[0, :, at : at + part] = dx.astype(BF16)
        g_in[...] += lax.dot_general(dpre, x, points, preferred_element_type=F32)
        g_out[...] += lax.dot_general(
            act_scr[:, at : at + part], dy, points, preferred_element_type=F32
        )

    width = x_ref.shape[2]
    gates(0)
    for at in range(part, width, part):
        gates(at)
        products(at - part)
    products(width - part)

    @pl.when(row == pl.num_programs(0) - 1)
    def _():
        parts, each, lanes = send_ref.shape
        shift = jnp.sum(g_bias[...], axis=1, keepdims=True)
        high = shift.astype(BF16).astype(F32)
        lane = lax.broadcasted_iota(jnp.int32, (HID, LANES), 1)
        tail = jnp.where(lane == 0, high, jnp.where(lane == 1, shift - high, tail_ref[...]))
        send = jnp.concatenate([g_in[...], g_out[...], tail], axis=1)
        send_ref[...] = send.reshape(parts, each, lanes).astype(BF16)


def mlp(x, dy, w_in, bias, w_out, tail, parts):
    rows, channels, columns = x.shape
    sources = dy.shape[0]
    whole = lambda shape: pl.BlockSpec(shape, lambda r: (0,) * len(shape))
    tile = pl.BlockSpec((1, channels, columns), lambda r: (r, 0, 0))
    send = (parts, HID // parts, 2 * channels + LANES)
    half = jnp.asarray(0.5, BF16)
    return pl.pallas_call(
        mlp_body,
        name="mlp",
        out_shape=(
            jax.ShapeDtypeStruct((rows, channels, columns), BF16),
            jax.ShapeDtypeStruct(send, BF16),
        ),
        grid=(rows,),
        in_specs=[
            tile,
            pl.BlockSpec((sources, None, 8, columns), lambda r: (0, r, 0, 0)),
            whole((HID, channels)),
            whole((channels, HID)),
            whole((HID, channels)),
            whole((HID, 1)),
            whole((HID, LANES)),
        ],
        out_specs=[tile, whole(send)],
        scratch_shapes=[
            pltpu.VMEM((HID, channels), F32),
            pltpu.VMEM((HID, channels), F32),
            pltpu.VMEM((HID, LANES), F32),
            pltpu.VMEM((HID, columns), BF16),
            pltpu.VMEM((HID, columns), BF16),
        ],
        compiler_params=pltpu.CompilerParams(dimension_semantics=("arbitrary",)),
    )(x, dy, w_in.T * half, w_in, w_out * half, 0.5 * bias[:, None], tail)


def shards(
    inputs, w_in, bias_in, w_out, advected, cotangent, offsets, stencil_row, stencil_col, fracs
):
    channels_dev, band_rows, columns = advected.shape
    row_blocks = band_rows // BH
    point_rows = inputs.shape[1]
    lat = lax.axis_size("lat")
    grp = lax.axis_size("grp")

    fracs = fracs.transpose(0, 2, 1)
    places = (
        offsets.transpose(0, 2, 1),
        stencil_row.T,
        stencil_col.T,
        catmull(fracs[0], fracs[1]),
    )
    head, tail = pack(places, cotangent, advected)
    top, bottom = exchange(head, tail)
    dy_band, edges = spread(places, cotangent)
    meta = jnp.stack([top[2 * channels_dev, 0, :LANES], bottom[2 * channels_dev, 0, :LANES]])
    dy_band = spread_edges(meta.astype(F32), top, bottom, edges, dy_band)
    dy_send = dy_band.reshape(grp, point_rows, channels_dev, columns)
    dy_points = lax.all_to_all(dy_send, "grp", split_axis=0, concat_axis=0, tiled=True)

    frac_parts = frac_sums(places, top, advected, bottom, cotangent)
    frac_local = jnp.sum(frac_parts, axis=(2, 3)).reshape(-1)
    parts = lat * grp
    each = HID // parts
    held = frac_local.shape[0] // each
    high = lax.reduce_precision(frac_local, 8, 7)
    both = jnp.stack([high.reshape(each, held), (frac_local - high).reshape(each, held)], axis=1)
    mine = jnp.where(jnp.arange(lat) == lax.axis_index("lat"), 1.0, 0.0)
    slots = mine[:, None, None, None] * both.reshape(1, 1, each, 2 * held)
    slots = jnp.broadcast_to(slots, (lat, grp, each, 2 * held)).reshape(HID, 2 * held)
    extra = jnp.pad(slots, ((0, 0), (held, LANES - 3 * held)))

    x_rows = inputs.transpose(1, 0, 2)
    dx_rows, send = mlp(x_rows, dy_points, w_in, bias_in, w_out, extra, parts)
    grad_inputs = dx_rows.transpose(1, 0, 2)

    got = lax.all_to_all(send, ("lat", "grp"), split_axis=0, concat_axis=0, tiled=True)
    total = jnp.sum(got.astype(F32), axis=0)
    scale = 1.0 / math.sqrt(point_rows * columns * parts)
    grad_first = total[:, :C].T * scale
    grad_second = total[:, C : 2 * C] * scale
    grad_shift = (total[:, 2 * C] + total[:, 2 * C + 1]) * scale
    total = total[:, 2 * C + held : 2 * C + 2 * held] + total[:, 2 * C + 2 * held : 2 * C + 3 * held]
    grad_frac = total.reshape(2, row_blocks, columns // BW) / math.sqrt(C * BH * BW)
    return (grad_inputs, grad_first, grad_shift, grad_second, grad_frac)


def solution(mesh):
    placed = (
        P(None, ("lat", "grp"), None),
        P(),
        P(),
        P(),
        P("grp", "lat", None),
        P("grp", "lat", None),
        P(None, "lat", None),
        P("lat", None),
        P("lat", None),
        P(None, "lat", None),
    )
    return jax.shard_map(
        shards,
        mesh=mesh,
        in_specs=placed,
        out_specs=(
            P(None, ("lat", "grp"), None),
            P(None, ("lat", "grp")),
            P(("lat", "grp")),
            P(("lat", "grp"), None),
            P(None, "lat", None),
        ),
        check_vma=False,
    )
```

```python
import functools
import math

import jax
import jax.numpy as jnp
from jax import lax
from jax.experimental import pallas as pl
from jax.experimental.pallas import tpu as pltpu
from jax.sharding import PartitionSpec as P

C = 256
BH = 16
BW = 256
LANES = 128
HID = 512
F32 = jnp.float32
BF16 = jnp.bfloat16


EDGE = 5


def weights(frac):
    square = frac * frac
    cube = square * frac
    return (
        0.5 * (-cube + 2.0 * square - frac),
        0.5 * (3.0 * cube - 5.0 * square + 2.0),
        0.5 * (-3.0 * cube + 4.0 * square + frac),
        0.5 * (cube - square),
    )


def slopes(frac):
    square = frac * frac
    return (
        0.5 * (-3.0 * square + 4.0 * frac - 1.0),
        0.5 * (9.0 * square - 10.0 * frac),
        0.5 * (-9.0 * square + 8.0 * frac + 1.0),
        0.5 * (3.0 * square - 2.0 * frac),
    )


def splat(value):
    return jnp.full((8, LANES), value, F32)


def exchange(head, tail):
    count = lax.axis_size("lat")
    above = lax.ppermute(tail, "lat", [(i, i + 1) for i in range(count - 1)])
    below = lax.ppermute(head, "lat", [(i + 1, i) for i in range(count - 1)])
    return above, below


def channel_minor():
    out = lax.broadcasted_iota(jnp.int32, (LANES, LANES), 0)
    src = lax.broadcasted_iota(jnp.int32, (LANES, LANES), 1)
    return ((out % 8) * 16 + out // 8 == src).astype(F32).astype(BF16)


def lanes():
    lane = lax.broadcasted_iota(jnp.int32, (8, LANES), 1)
    return lane, lax.broadcasted_iota(jnp.int32, (8, LANES), 0)


def col_taps(values, shift):
    lane, row = lanes()
    base = jnp.zeros((8, LANES), F32)
    for tap in range(4):
        base = jnp.where(lane - row == tap, values[tap], base)
    left, right = [], []
    for group in range(0, LANES, 8):
        moved = pltpu.roll(base, (shift + group) & (LANES - 1), 1)
        inside = lane - row >= shift + group
        left.append(jnp.where(inside, moved, 0.0))
        right.append(jnp.where(inside, 0.0, moved))
    both = [jnp.concatenate(left, axis=0), jnp.concatenate(right, axis=0)]
    return jnp.concatenate(both, axis=1).astype(BF16)


REACH = BH + 4


def row_taps(values):
    lane, row = lanes()
    base = jnp.zeros((8, LANES), F32)
    for tap in range(4):
        base = jnp.where((lane - BH * row + tap) & (LANES - 1) == 0, values[tap], base)
    own = lane // BH == row
    moved = [base] + [pltpu.roll(base, step, 1) for step in range(1, REACH)]
    return jnp.concatenate([jnp.where(own, part, 0.0) for part in moved], axis=0).astype(BF16)


def pack_body(offs, srow, scol, fracs, cot, adv, head_ref, tail_ref, rows, meta, arrived, left):
    channels = cot.shape[0]
    last = offs.shape[2] - 1
    inward, outward = [], []
    for side, (out_ref, row) in enumerate(((head_ref, 0), (tail_ref, last))):
        for which, source in enumerate((cot, adv)):
            job = 2 * side + which
            inward.append(
                pltpu.make_async_copy(
                    source.at[:, row * BH : (row + 1) * BH, :], rows.at[job], arrived.at[job]
                )
            )
            place = slice(which * channels, (which + 1) * channels)
            outward.append(
                pltpu.make_async_copy(rows.at[job], out_ref.at[place], left.at[job])
            )
    for job in inward:
        job.start()
    lane = lax.broadcasted_iota(jnp.int32, (BH, LANES), 1)
    for side, (out_ref, row) in enumerate(((head_ref, 0), (tail_ref, last))):
        value = jnp.zeros((BH, LANES), F32)
        for block in range(4):
            own = [
                (BH // 2 * offs[0, block, row] + srow[block, row]).astype(F32),
                offs[1, block, row].astype(F32),
                scol[block, row].astype(F32),
                fracs[0, block, row],
                fracs[1, block, row],
            ]
            for slot, entry in enumerate(own):
                value = jnp.where(lane == block * EDGE + slot, entry, value)
        meta[side] = jnp.zeros(meta.shape[1:], BF16)
        for part in range(3):
            high = value.astype(BF16)
            meta[side, :, part * LANES : (part + 1) * LANES] = high
            value = value - high.astype(F32)
        outward.append(
            pltpu.make_async_copy(meta.at[side], out_ref.at[2 * channels], left.at[4 + side])
        )
        outward[-1].start()
    for job in range(4):
        inward[job].wait()
        outward[job].start()
    for job in outward:
        job.wait()


def pack(places, cot, adv):
    channels, band_rows, columns = cot.shape
    shape = jax.ShapeDtypeStruct((2 * channels + 1, BH, columns), BF16)
    anywhere = pl.BlockSpec(memory_space=pl.ANY)
    return pl.pallas_call(
        pack_body,
        name="pack",
        out_shape=(shape, shape),
        grid_spec=pltpu.PrefetchScalarGridSpec(
            num_scalar_prefetch=4,
            grid=(1,),
            in_specs=[anywhere, anywhere],
            out_specs=[anywhere, anywhere],
            scratch_shapes=[
                pltpu.VMEM((4, channels, BH, columns), BF16),
                pltpu.VMEM((2, BH, columns), BF16),
                pltpu.SemaphoreType.DMA((4,)),
                pltpu.SemaphoreType.DMA((6,)),
            ],
        ),
        compiler_params=pltpu.CompilerParams(dimension_semantics=("arbitrary",)),
    )(*places, cot, adv)


def spread_blocks(jobs, tap_scr, row_scr, z_scr, acc):
    for job, (rows, block, first, py, tile, shift, wx, wy) in enumerate(jobs):
        tap_scr[job] = col_taps(wx, shift)
        row_scr[job] = row_taps(wy)
    for job, (rows, block, first, py, tile, shift, wx, wy) in enumerate(jobs):
        z = jnp.dot(halves_of(rows, block), tap_scr[job], preferred_element_type=F32)
        z_scr[job, :, 0:LANES] = z[0:LANES, 0:LANES].astype(BF16)
        middle = z[0:LANES, LANES:] + z[LANES:, 0:LANES]
        z_scr[job, :, LANES : 2 * LANES] = middle.astype(BF16)
        z_scr[job, :, 2 * LANES :] = z[LANES:, LANES:].astype(BF16)
    moved = [
        jnp.dot(row_scr[job], z_scr[job], preferred_element_type=F32) for job in range(len(jobs))
    ]
    for job, (rows, block, first, py, tile, shift, wx, wy) in enumerate(jobs):
        for part in range(3):
            target = (2 * block + 6 + part + tile) & 7
            value = moved[job][:, part * LANES : (part + 1) * LANES].reshape(REACH, 8, LANES)
            at = pl.ds(first + py, REACH)
            acc[at, target] = acc[at, target] + value


def spread_scratch():
    return [
        pltpu.VMEM((8, LANES, 2 * LANES), BF16),
        pltpu.VMEM((8, REACH * 8, LANES), BF16),
        pltpu.VMEM((8, LANES, 3 * LANES), BF16),
    ]


def halves_of(rows, block):
    return jnp.concatenate(
        [
            rows[:, block * BW : block * BW + LANES],
            rows[:, block * BW + LANES : (block + 1) * BW],
        ],
        axis=0,
    )


def emit(acc, first, out_ref):
    for tile_index in range(8):
        done = acc[pl.ds(first, BH), tile_index].reshape(BH * 8, LANES)
        out_ref[:, tile_index * LANES : (tile_index + 1) * LANES] = done.astype(BF16)


def spread_body(offs, srow, scol, fracs, cot_ref, out_ref, edge_ref, tap_scr, row_scr, z_scr, acc):
    step = pl.program_id(0)
    last = pl.num_programs(0) - 1

    @pl.when(step == 0)
    def _():
        acc[0 : 2 * BH] = jnp.zeros((2 * BH,) + acc.shape[1:], F32)

    @pl.when(step < last)
    def _():
        acc[pl.ds((2 * step + 2) * BH, 2 * BH)] = jnp.zeros((2 * BH,) + acc.shape[1:], F32)
        jobs = []
        for half in range(2):
            row = 2 * step + half
            rows = cot_ref[:, half * BH : (half + 1) * BH].reshape(LANES, cot_ref.shape[2])
            for block in range(4):
                jobs.append(
                    (
                        rows,
                        block,
                        row * BH,
                        BH // 2 * offs[0, block, row] + srow[block, row],
                        offs[1, block, row],
                        scol[block, row],
                        weights(splat(fracs[1, block, row])),
                        weights(splat(fracs[0, block, row])),
                    )
                )
        spread_blocks(jobs, tap_scr, row_scr, z_scr, acc)

    emit(acc, jnp.maximum(2 * step - 1, 0) * BH, out_ref.at[0])
    emit(acc, 2 * step * BH, out_ref.at[1])

    @pl.when(step == 0)
    def _():
        edge_ref[0] = acc[BH : 2 * BH]

    @pl.when(step == last)
    def _():
        edge_ref[0] = acc[pl.ds(2 * last * BH, BH)]


def spread(places, cot):
    channels, band_rows, columns = cot.shape
    blocks = band_rows // BH
    pairs = blocks // 2
    tiles = columns // LANES
    return pl.pallas_call(
        spread_body,
        name="spread",
        out_shape=(
            jax.ShapeDtypeStruct((blocks, BH * channels, columns), BF16),
            jax.ShapeDtypeStruct((2, BH, tiles, channels, LANES), F32),
        ),
        grid_spec=pltpu.PrefetchScalarGridSpec(
            num_scalar_prefetch=4,
            grid=(pairs + 1,),
            in_specs=[
                pl.BlockSpec(
                    (channels, 2 * BH, columns), lambda g, *a: (0, jnp.minimum(g, pairs - 1), 0)
                )
            ],
            out_specs=[
                pl.BlockSpec(
                    (2, BH * channels, columns), lambda g, *a: (jnp.maximum(g - 1, 0), 0, 0)
                ),
                pl.BlockSpec(
                    (1, BH, tiles, channels, LANES),
                    lambda g, *a: (jnp.where(g == pairs, 1, 0), 0, 0, 0, 0),
                ),
            ],
            scratch_shapes=spread_scratch()
            + [pltpu.VMEM(((blocks + 2) * BH, tiles, channels, LANES), F32)],
        ),
        compiler_params=pltpu.CompilerParams(dimension_semantics=("arbitrary",)),
    )(*places, cot)


def edge_body(meta, top_ref, bot_ref, edge_ref, whole, out_ref, tap_scr, row_scr, z_scr, acc):
    step = pl.program_id(0)
    upper, lower = 2 * BH, 3 * BH

    @pl.when(step == 0)
    def _():
        acc[0:upper] = jnp.zeros((upper,) + acc.shape[1:], F32)
        acc[upper : upper + BH] = edge_ref[0]
        acc[lower : lower + BH] = edge_ref[1]
        acc[lower + BH :] = jnp.zeros((2 * BH,) + acc.shape[1:], F32)
        jobs = []
        for side, ref in enumerate((top_ref, bot_ref)):
            rows = ref[0 : LANES // BH].reshape(LANES, ref.shape[2])
            for block in range(4):
                at = [block * EDGE + slot for slot in range(EDGE)]
                place = [meta[side, k].astype(jnp.int32) for k in at[:3]]
                fracs = [
                    meta[side, k] + meta[side, LANES + k] + meta[side, 2 * LANES + k]
                    for k in at[3:]
                ]
                wy, wx = [weights(splat(frac)) for frac in fracs]
                jobs.append((rows, block, side * lower, *place, wx, wy))
        spread_blocks(jobs, tap_scr, row_scr, z_scr, acc)

    emit(acc, upper + step * BH, out_ref.at[0])


def spread_edges(meta, top, bottom, edges, dy):
    blocks, rows, columns = dy.shape
    channels = edges.shape[3]
    return pl.pallas_call(
        edge_body,
        name="spread_edges",
        out_shape=jax.ShapeDtypeStruct(dy.shape, dy.dtype),
        grid_spec=pltpu.PrefetchScalarGridSpec(
            num_scalar_prefetch=1,
            grid=(2,),
            in_specs=[
                pl.BlockSpec(memory_space=pltpu.VMEM),
                pl.BlockSpec(memory_space=pltpu.VMEM),
                pl.BlockSpec(edges.shape, lambda g, a: (0, 0, 0, 0, 0)),
                pl.BlockSpec(memory_space=pl.ANY),
            ],
            out_specs=pl.BlockSpec((1, rows, columns), lambda g, a: (g * (blocks - 1), 0, 0)),
            scratch_shapes=spread_scratch() + [pltpu.VMEM((6 * BH,) + edges.shape[2:], F32)],
        ),
        input_output_aliases={4: 0},
        compiler_params=pltpu.CompilerParams(dimension_semantics=("arbitrary",)),
    )(meta, top, bottom, edges, dy)


def frac_body(
    offs, srow, scol, fracs, top_ref, mid_ref, next_ref, bot_ref, cot_ref, out_ref, cot_scr, z_scr, field
):
    step = pl.program_id(0)
    last = pl.num_programs(0) - 1
    width = cot_scr.shape[1]
    order = channel_minor()

    def put(row_block, source):
        rows = source[...].reshape(LANES, width)
        moved = jnp.dot(order, rows, preferred_element_type=F32)
        for tile_index in range(8):
            field[pl.ds(row_block * BH, BH), tile_index] = moved[
                :, tile_index * LANES : (tile_index + 1) * LANES
            ].reshape(BH, 8, LANES)

    @pl.when(step == 0)
    def _():
        put(0, top_ref)
        put(1, mid_ref)

    @pl.when(step == last)
    def _():
        put(step + 2, bot_ref)

    @pl.when(step < last)
    def _():
        put(step + 2, next_ref)

    rows = cot_ref[...].reshape(LANES, width)
    cot_scr[...] = jnp.dot(order, rows, preferred_element_type=F32).astype(BF16)
    for block in range(4):
        py = BH // 2 * offs[0, block, step] + srow[block, step]
        tile = offs[1, block, step]
        shift = scol[block, step]
        row_frac, col_frac = splat(fracs[0, block, step]), splat(fracs[1, block, step])
        both = jnp.concatenate(
            [
                col_taps(weights(col_frac), shift),
                col_taps(slopes(col_frac), shift),
            ],
            axis=1,
        )
        halves = jnp.concatenate(
            [
                cot_scr[:, block * BW : block * BW + LANES],
                cot_scr[:, block * BW + LANES : (block + 1) * BW],
            ],
            axis=0,
        )
        z_scr[block] = jnp.dot(halves, both, preferred_element_type=F32)
        by_value = [jnp.zeros((8, LANES), F32) for tap in range(4)]
        by_slope = [jnp.zeros((8, LANES), F32) for tap in range(4)]
        for part in range(3):
            pair = []
            for lane in (0, 2 * LANES):
                if part == 0:
                    z = z_scr[block, 0:LANES, lane : lane + LANES]
                elif part == 1:
                    z = (
                        z_scr[block, 0:LANES, lane + LANES : lane + 2 * LANES]
                        + z_scr[block, LANES:, lane : lane + LANES]
                    )
                else:
                    z = z_scr[block, LANES:, lane + LANES : lane + 2 * LANES]
                pair.append(z.reshape(BH, 8, LANES))
            source = (2 * block + 6 + part + tile) & 7
            for j in range(BH + 3):
                value = field[step * BH + py + j, source]
                for tap in range(4):
                    if 0 <= j - tap < BH:
                        by_value[tap] = by_value[tap] + value * pair[0][j - tap]
                        by_slope[tap] = by_slope[tap] + value * pair[1][j - tap]
        first = jnp.zeros((8, LANES), F32)
        second = jnp.zeros((8, LANES), F32)
        wy, sy = weights(row_frac), slopes(row_frac)
        for tap in range(4):
            first = first + sy[tap].astype(BF16).astype(F32) * by_value[tap]
            second = second + wy[tap].astype(BF16).astype(F32) * by_slope[tap]
        out_ref[0, block] = first
        out_ref[1, block] = second


def frac_sums(places, top, field, bottom, cot):
    channels, band_rows, columns = cot.shape
    blocks = band_rows // BH
    shape = (channels, BH, columns)
    return pl.pallas_call(
        frac_body,
        name="frac_sums",
        out_shape=jax.ShapeDtypeStruct((2, blocks * 4, 8, LANES), F32),
        grid_spec=pltpu.PrefetchScalarGridSpec(
            num_scalar_prefetch=4,
            grid=(blocks,),
            in_specs=[
                pl.BlockSpec(shape, lambda g, *a: (1, 0, 0)),
                pl.BlockSpec(shape, lambda g, *a: (0, 0, 0)),
                pl.BlockSpec(shape, lambda g, *a: (0, jnp.minimum(g + 1, blocks - 1), 0)),
                pl.BlockSpec(shape, lambda g, *a: (1, 0, 0)),
                pl.BlockSpec(shape, lambda g, *a: (0, g, 0)),
            ],
            out_specs=pl.BlockSpec((2, 4, 8, LANES), lambda g, *a: (0, g, 0, 0)),
            scratch_shapes=[
                pltpu.VMEM((BH * channels, columns), BF16),
                pltpu.VMEM((4, 2 * LANES, 4 * LANES), F32),
                pltpu.VMEM(((blocks + 2) * BH, columns // LANES, channels, LANES), F32),
            ],
        ),
        compiler_params=pltpu.CompilerParams(dimension_semantics=("arbitrary",)),
    )(*places, top, field, field, bottom, cot)


def mlp_body(
    x_ref, dy_ref, w_in_t, w_in, w_out, half_bias, tail_ref, dx_ref, send_ref, g_in, g_out, g_bias,
    act_scr, dpre_scr
):
    row = pl.program_id(0)

    @pl.when(row == 0)
    def _():
        g_in[...] = jnp.zeros_like(g_in)
        g_out[...] = jnp.zeros_like(g_out)
        g_bias[...] = jnp.zeros_like(g_bias)

    part = 256
    points = (((1,), (1,)), ((), ()))

    def gates(at):
        x = x_ref[0, :, at : at + part]
        dy = dy_ref[:, :, at : at + part].reshape(C, part)
        half = jnp.dot(w_in_t[...], x, preferred_element_type=F32) + half_bias[...]
        twice = 1.0 + jnp.tanh(half)
        act = half * twice
        dact = jnp.dot(w_out[...], dy, preferred_element_type=F32)
        dpre = (dact * (twice + act * (2.0 - twice))).astype(BF16)
        act_scr[:, at : at + part] = act.astype(BF16)
        dpre_scr[:, at : at + part] = dpre
        total = g_bias[...]
        for lane in range(0, part, LANES):
            total = total + dpre[:, lane : lane + LANES].astype(F32)
        g_bias[...] = total

    def products(at):
        x = x_ref[0, :, at : at + part]
        dy = dy_ref[:, :, at : at + part].reshape(C, part)
        dpre = dpre_scr[:, at : at + part]
        dx = dy.astype(F32) + jnp.dot(w_in[...], dpre, preferred_element_type=F32)
        dx_ref[0, :, at : at + part] = dx.astype(BF16)
        g_in[...] += lax.dot_general(dpre, x, points, preferred_element_type=F32)
        g_out[...] += lax.dot_general(
            act_scr[:, at : at + part], dy, points, preferred_element_type=F32
        )

    width = x_ref.shape[2]
    gates(0)
    for at in range(part, width, part):
        gates(at)
        products(at - part)
    products(width - part)

    @pl.when(row == pl.num_programs(0) - 1)
    def _():
        parts, each, lanes = send_ref.shape
        shift = jnp.sum(g_bias[...], axis=1, keepdims=True)
        high = shift.astype(BF16).astype(F32)
        lane = lax.broadcasted_iota(jnp.int32, (HID, LANES), 1)
        tail = jnp.where(lane == 0, high, jnp.where(lane == 1, shift - high, tail_ref[...]))
        send = jnp.concatenate([g_in[...], g_out[...], tail], axis=1)
        send_ref[...] = send.reshape(parts, each, lanes).astype(BF16)


def mlp(x, dy, w_in, bias, w_out, tail, parts):
    rows, channels, columns = x.shape
    sources = dy.shape[0]
    whole = lambda shape: pl.BlockSpec(shape, lambda r: (0,) * len(shape))
    tile = pl.BlockSpec((1, channels, columns), lambda r: (r, 0, 0))
    send = (parts, HID // parts, 2 * channels + LANES)
    half = jnp.asarray(0.5, BF16)
    return pl.pallas_call(
        mlp_body,
        name="mlp",
        out_shape=(
            jax.ShapeDtypeStruct((rows, channels, columns), BF16),
            jax.ShapeDtypeStruct(send, BF16),
        ),
        grid=(rows,),
        in_specs=[
            tile,
            pl.BlockSpec((sources, None, 8, columns), lambda r: (0, r, 0, 0)),
            whole((HID, channels)),
            whole((channels, HID)),
            whole((HID, channels)),
            whole((HID, 1)),
            whole((HID, LANES)),
        ],
        out_specs=[tile, whole(send)],
        scratch_shapes=[
            pltpu.VMEM((HID, channels), F32),
            pltpu.VMEM((HID, channels), F32),
            pltpu.VMEM((HID, LANES), F32),
            pltpu.VMEM((HID, columns), BF16),
            pltpu.VMEM((HID, columns), BF16),
        ],
        compiler_params=pltpu.CompilerParams(dimension_semantics=("arbitrary",)),
    )(x, dy, w_in.T * half, w_in, w_out * half, 0.5 * bias[:, None], tail)


def finish_body(scale, frac_scale, got_ref, first_ref, second_ref, shift_ref, frac_ref):
    total = jnp.sum(got_ref[...].astype(F32), axis=0)
    each = total.shape[0]
    held = 2 * frac_ref.shape[2]
    first_ref[...] = total[:, 0:C] * scale
    second_ref[...] = total[:, C : 2 * C] * scale
    tail = total[:, 2 * C :]
    lane = lax.broadcasted_iota(jnp.int32, (each, LANES), 1)
    row = lax.broadcasted_iota(jnp.int32, (each, LANES), 0)
    shift = tail[:, 0:1] + tail[:, 1:2]
    shift = jnp.sum(jnp.where(lane == row, shift, 0.0), axis=0, keepdims=True)
    shift_ref[...] = shift[:, 0:each] * scale
    frac = tail[:, held : 2 * held] + tail[:, 2 * held : 3 * held]
    half = held // 2
    frac_ref[0] = frac[:, 0:half] * frac_scale
    frac_ref[1] = frac[:, half:] * frac_scale


def finish(got, scale, frac_scale, row_blocks):
    each = got.shape[1]
    return pl.pallas_call(
        functools.partial(finish_body, scale, frac_scale),
        name="finish",
        out_shape=(
            jax.ShapeDtypeStruct((each, C), F32),
            jax.ShapeDtypeStruct((each, C), F32),
            jax.ShapeDtypeStruct((1, each), F32),
            jax.ShapeDtypeStruct((2, each, row_blocks), F32),
        ),
        in_specs=[pl.BlockSpec(memory_space=pltpu.VMEM)],
    )(got)


def shards(
    inputs, w_in, bias_in, w_out, advected, cotangent, offsets, stencil_row, stencil_col, fracs
):
    channels_dev, band_rows, columns = advected.shape
    row_blocks = band_rows // BH
    point_rows = inputs.shape[1]
    lat = lax.axis_size("lat")
    grp = lax.axis_size("grp")

    places = (
        offsets.transpose(0, 2, 1),
        stencil_row.T,
        stencil_col.T,
        fracs.transpose(0, 2, 1),
    )
    head, tail = pack(places, cotangent, advected)
    top, bottom = exchange(head, tail)
    dy_band, edges = spread(places, cotangent)
    meta = jnp.stack([halo[2 * channels_dev, 0, : 3 * LANES] for halo in (top, bottom)])
    dy_band = spread_edges(meta.astype(F32), top, bottom, edges, dy_band)
    dy_send = dy_band.reshape(grp, point_rows, channels_dev, columns)
    dy_points = lax.all_to_all(dy_send, "grp", split_axis=0, concat_axis=0, tiled=True)

    frac_parts = frac_sums(places, top, advected, bottom, cotangent)
    parts = lat * grp
    each = HID // parts
    held = 2 * row_blocks
    frac_local = jnp.sum(frac_parts, axis=(2, 3)).reshape(held, columns // BW).T
    high = lax.reduce_precision(frac_local, 8, 7)
    both = jnp.stack([high, frac_local - high], axis=1)
    mine = jnp.where(jnp.arange(lat) == lax.axis_index("lat"), 1.0, 0.0)
    slots = mine[:, None, None, None] * both.reshape(1, 1, each, 2 * held)
    slots = jnp.broadcast_to(slots, (lat, grp, each, 2 * held)).reshape(HID, 2 * held)
    extra = jnp.pad(slots, ((0, 0), (held, LANES - 3 * held)))

    x_rows = inputs.transpose(1, 0, 2)
    dx_rows, send = mlp(x_rows, dy_points, w_in, bias_in, w_out, extra, parts)
    grad_inputs = dx_rows.transpose(1, 0, 2)

    got = lax.all_to_all(send, ("lat", "grp"), split_axis=0, concat_axis=0, tiled=True)
    scale = 1.0 / math.sqrt(point_rows * columns * parts)
    first, second, shift, frac = finish(got, scale, 1.0 / math.sqrt(C * BH * BW), row_blocks)
    return (grad_inputs, first.T, shift.reshape(each), second, frac.transpose(0, 2, 1))


def solution(mesh):
    placed = (
        P(None, ("lat", "grp"), None),
        P(),
        P(),
        P(),
        P("grp", "lat", None),
        P("grp", "lat", None),
        P(None, "lat", None),
        P("lat", None),
        P("lat", None),
        P(None, "lat", None),
    )
    return jax.shard_map(
        shards,
        mesh=mesh,
        in_specs=placed,
        out_specs=(
            P(None, ("lat", "grp"), None),
            P(None, ("lat", "grp")),
            P(("lat", "grp")),
            P(("lat", "grp"), None),
            P(None, "lat", None),
        ),
        check_vma=False,
    )
```

```python
import functools
import math

import jax
import jax.numpy as jnp
from jax import lax
from jax.experimental import pallas as pl
from jax.experimental.pallas import tpu as pltpu
from jax.sharding import PartitionSpec as P

C = 256
BH = 16
BW = 256
LANES = 128
HID = 512
F32 = jnp.float32
BF16 = jnp.bfloat16


EDGE = 5


def weights(frac):
    square = frac * frac
    cube = square * frac
    return (
        0.5 * (-cube + 2.0 * square - frac),
        0.5 * (3.0 * cube - 5.0 * square + 2.0),
        0.5 * (-3.0 * cube + 4.0 * square + frac),
        0.5 * (cube - square),
    )


def slopes(frac):
    square = frac * frac
    return (
        0.5 * (-3.0 * square + 4.0 * frac - 1.0),
        0.5 * (9.0 * square - 10.0 * frac),
        0.5 * (-9.0 * square + 8.0 * frac + 1.0),
        0.5 * (3.0 * square - 2.0 * frac),
    )


def splat(value):
    return jnp.full((8, LANES), value, F32)


def exchange(head, tail):
    count = lax.axis_size("lat")
    above = lax.ppermute(tail, "lat", [(i, i + 1) for i in range(count - 1)])
    below = lax.ppermute(head, "lat", [(i + 1, i) for i in range(count - 1)])
    return above, below


def channel_minor():
    out = lax.broadcasted_iota(jnp.int32, (LANES, LANES), 0)
    src = lax.broadcasted_iota(jnp.int32, (LANES, LANES), 1)
    return ((out % 8) * 16 + out // 8 == src).astype(F32).astype(BF16)


def lanes():
    lane = lax.broadcasted_iota(jnp.int32, (8, LANES), 1)
    return lane, lax.broadcasted_iota(jnp.int32, (8, LANES), 0)


def col_taps(values, shift):
    lane, row = lanes()
    base = jnp.zeros((8, LANES), F32)
    for tap in range(4):
        base = jnp.where(lane - row == tap, values[tap], base)
    left, right = [], []
    for group in range(0, LANES, 8):
        moved = pltpu.roll(base, (shift + group) & (LANES - 1), 1)
        inside = lane - row >= shift + group
        left.append(jnp.where(inside, moved, 0.0))
        right.append(jnp.where(inside, 0.0, moved))
    both = [jnp.concatenate(left, axis=0), jnp.concatenate(right, axis=0)]
    return jnp.concatenate(both, axis=1).astype(BF16)


REACH = BH + 4


def row_taps(values):
    lane, row = lanes()
    base = jnp.zeros((8, LANES), F32)
    for tap in range(4):
        base = jnp.where((lane - BH * row + tap) & (LANES - 1) == 0, values[tap], base)
    own = lane // BH == row
    moved = [base] + [pltpu.roll(base, step, 1) for step in range(1, REACH)]
    return jnp.concatenate([jnp.where(own, part, 0.0) for part in moved], axis=0).astype(BF16)


def pack_body(offs, srow, scol, fracs, cot, adv, head_ref, tail_ref, rows, meta, arrived, left):
    channels = cot.shape[0]
    last = offs.shape[2] - 1
    inward, outward = [], []
    for side, (out_ref, row) in enumerate(((head_ref, 0), (tail_ref, last))):
        for which, source in enumerate((cot, adv)):
            job = 2 * side + which
            inward.append(
                pltpu.make_async_copy(
                    source.at[:, row * BH : (row + 1) * BH, :], rows.at[job], arrived.at[job]
                )
            )
            place = slice(which * channels, (which + 1) * channels)
            outward.append(
                pltpu.make_async_copy(rows.at[job], out_ref.at[place], left.at[job])
            )
    for job in inward:
        job.start()
    lane = lax.broadcasted_iota(jnp.int32, (BH, LANES), 1)
    for side, (out_ref, row) in enumerate(((head_ref, 0), (tail_ref, last))):
        value = jnp.zeros((BH, LANES), F32)
        for block in range(4):
            own = [
                (BH // 2 * offs[0, block, row] + srow[block, row]).astype(F32),
                offs[1, block, row].astype(F32),
                scol[block, row].astype(F32),
                fracs[0, block, row],
                fracs[1, block, row],
            ]
            for slot, entry in enumerate(own):
                value = jnp.where(lane == block * EDGE + slot, entry, value)
        meta[side] = jnp.zeros(meta.shape[1:], BF16)
        for part in range(3):
            high = value.astype(BF16)
            meta[side, :, part * LANES : (part + 1) * LANES] = high
            value = value - high.astype(F32)
        outward.append(
            pltpu.make_async_copy(meta.at[side], out_ref.at[2 * channels], left.at[4 + side])
        )
        outward[-1].start()
    for job in range(4):
        inward[job].wait()
        outward[job].start()
    for job in outward:
        job.wait()


def pack(places, cot, adv):
    channels, band_rows, columns = cot.shape
    shape = jax.ShapeDtypeStruct((2 * channels + 1, BH, columns), BF16)
    anywhere = pl.BlockSpec(memory_space=pl.ANY)
    return pl.pallas_call(
        pack_body,
        name="pack",
        out_shape=(shape, shape),
        grid_spec=pltpu.PrefetchScalarGridSpec(
            num_scalar_prefetch=4,
            grid=(1,),
            in_specs=[anywhere, anywhere],
            out_specs=[anywhere, anywhere],
            scratch_shapes=[
                pltpu.VMEM((4, channels, BH, columns), BF16),
                pltpu.VMEM((2, BH, columns), BF16),
                pltpu.SemaphoreType.DMA((4,)),
                pltpu.SemaphoreType.DMA((6,)),
            ],
        ),
        compiler_params=pltpu.CompilerParams(dimension_semantics=("arbitrary",)),
    )(*places, cot, adv)


def spread_blocks(jobs, tap_scr, row_scr, z_scr, acc):
    for job, (rows, block, first, py, tile, shift, wx, wy) in enumerate(jobs):
        tap_scr[job] = col_taps(wx, shift)
        row_scr[job] = row_taps(wy)
    for job, (rows, block, first, py, tile, shift, wx, wy) in enumerate(jobs):
        z = jnp.dot(halves_of(rows, block), tap_scr[job], preferred_element_type=F32)
        z_scr[job, :, 0:LANES] = z[0:LANES, 0:LANES].astype(BF16)
        middle = z[0:LANES, LANES:] + z[LANES:, 0:LANES]
        z_scr[job, :, LANES : 2 * LANES] = middle.astype(BF16)
        z_scr[job, :, 2 * LANES :] = z[LANES:, LANES:].astype(BF16)
    moved = [
        jnp.dot(row_scr[job], z_scr[job], preferred_element_type=F32) for job in range(len(jobs))
    ]
    for job, (rows, block, first, py, tile, shift, wx, wy) in enumerate(jobs):
        for part in range(3):
            target = (2 * block + 6 + part + tile) & 7
            value = moved[job][:, part * LANES : (part + 1) * LANES].reshape(REACH, 8, LANES)
            at = pl.ds(first + py, REACH)
            acc[at, target] = acc[at, target] + value


def spread_scratch():
    return [
        pltpu.VMEM((8, LANES, 2 * LANES), BF16),
        pltpu.VMEM((8, REACH * 8, LANES), BF16),
        pltpu.VMEM((8, LANES, 3 * LANES), BF16),
    ]


def halves_of(rows, block):
    return jnp.concatenate(
        [
            rows[:, block * BW : block * BW + LANES],
            rows[:, block * BW + LANES : (block + 1) * BW],
        ],
        axis=0,
    )


def emit(acc, first, out_ref):
    for tile_index in range(8):
        done = acc[pl.ds(first, BH), tile_index].reshape(BH * 8, LANES)
        out_ref[:, tile_index * LANES : (tile_index + 1) * LANES] = done.astype(BF16)


def spread_body(offs, srow, scol, fracs, cot_ref, out_ref, edge_ref, tap_scr, row_scr, z_scr, acc):
    step = pl.program_id(0)
    last = pl.num_programs(0) - 1

    @pl.when(step == 0)
    def _():
        acc[0 : 2 * BH] = jnp.zeros((2 * BH,) + acc.shape[1:], F32)

    @pl.when(step < last)
    def _():
        acc[pl.ds((2 * step + 2) * BH, 2 * BH)] = jnp.zeros((2 * BH,) + acc.shape[1:], F32)
        jobs = []
        for half in range(2):
            row = 2 * step + half
            rows = cot_ref[:, half * BH : (half + 1) * BH].reshape(LANES, cot_ref.shape[2])
            for block in range(4):
                jobs.append(
                    (
                        rows,
                        block,
                        row * BH,
                        BH // 2 * offs[0, block, row] + srow[block, row],
                        offs[1, block, row],
                        scol[block, row],
                        weights(splat(fracs[1, block, row])),
                        weights(splat(fracs[0, block, row])),
                    )
                )
        spread_blocks(jobs, tap_scr, row_scr, z_scr, acc)

    emit(acc, jnp.maximum(2 * step - 1, 0) * BH, out_ref.at[0])
    emit(acc, 2 * step * BH, out_ref.at[1])

    @pl.when(step == 0)
    def _():
        edge_ref[0] = acc[BH : 2 * BH]

    @pl.when(step == last)
    def _():
        edge_ref[0] = acc[pl.ds(2 * last * BH, BH)]


def spread(places, cot):
    channels, band_rows, columns = cot.shape
    blocks = band_rows // BH
    pairs = blocks // 2
    tiles = columns // LANES
    return pl.pallas_call(
        spread_body,
        name="spread",
        out_shape=(
            jax.ShapeDtypeStruct((blocks, BH * channels, columns), BF16),
            jax.ShapeDtypeStruct((2, BH, tiles, channels, LANES), F32),
        ),
        grid_spec=pltpu.PrefetchScalarGridSpec(
            num_scalar_prefetch=4,
            grid=(pairs + 1,),
            in_specs=[
                pl.BlockSpec(
                    (channels, 2 * BH, columns), lambda g, *a: (0, jnp.minimum(g, pairs - 1), 0)
                )
            ],
            out_specs=[
                pl.BlockSpec(
                    (2, BH * channels, columns), lambda g, *a: (jnp.maximum(g - 1, 0), 0, 0)
                ),
                pl.BlockSpec(
                    (1, BH, tiles, channels, LANES),
                    lambda g, *a: (jnp.where(g == pairs, 1, 0), 0, 0, 0, 0),
                ),
            ],
            scratch_shapes=spread_scratch()
            + [pltpu.VMEM(((blocks + 2) * BH, tiles, channels, LANES), F32)],
        ),
        compiler_params=pltpu.CompilerParams(dimension_semantics=("arbitrary",)),
    )(*places, cot)


def edge_body(meta, top_ref, bot_ref, edge_ref, whole, out_ref, tap_scr, row_scr, z_scr, acc):
    step = pl.program_id(0)
    upper, lower = 2 * BH, 3 * BH

    @pl.when(step == 0)
    def _():
        acc[0:upper] = jnp.zeros((upper,) + acc.shape[1:], F32)
        acc[upper : upper + BH] = edge_ref[0]
        acc[lower : lower + BH] = edge_ref[1]
        acc[lower + BH :] = jnp.zeros((2 * BH,) + acc.shape[1:], F32)
        jobs = []
        for side, ref in enumerate((top_ref, bot_ref)):
            rows = ref[0 : LANES // BH].reshape(LANES, ref.shape[2])
            for block in range(4):
                at = [block * EDGE + slot for slot in range(EDGE)]
                place = [meta[side, k].astype(jnp.int32) for k in at[:3]]
                fracs = [
                    meta[side, k] + meta[side, LANES + k] + meta[side, 2 * LANES + k]
                    for k in at[3:]
                ]
                wy, wx = [weights(splat(frac)) for frac in fracs]
                jobs.append((rows, block, side * lower, *place, wx, wy))
        spread_blocks(jobs, tap_scr, row_scr, z_scr, acc)

    emit(acc, upper + step * BH, out_ref.at[0])


def spread_edges(meta, top, bottom, edges, dy):
    blocks, rows, columns = dy.shape
    channels = edges.shape[3]
    return pl.pallas_call(
        edge_body,
        name="spread_edges",
        out_shape=jax.ShapeDtypeStruct(dy.shape, dy.dtype),
        grid_spec=pltpu.PrefetchScalarGridSpec(
            num_scalar_prefetch=1,
            grid=(2,),
            in_specs=[
                pl.BlockSpec(memory_space=pltpu.VMEM),
                pl.BlockSpec(memory_space=pltpu.VMEM),
                pl.BlockSpec(edges.shape, lambda g, a: (0, 0, 0, 0, 0)),
                pl.BlockSpec(memory_space=pl.ANY),
            ],
            out_specs=pl.BlockSpec((1, rows, columns), lambda g, a: (g * (blocks - 1), 0, 0)),
            scratch_shapes=spread_scratch() + [pltpu.VMEM((6 * BH,) + edges.shape[2:], F32)],
        ),
        input_output_aliases={4: 0},
        compiler_params=pltpu.CompilerParams(dimension_semantics=("arbitrary",)),
    )(meta, top, bottom, edges, dy)


def frac_body(
    offs, srow, scol, fracs, top_ref, mid_ref, next_ref, bot_ref, cot_ref, out_ref, cot_scr, z_scr, field
):
    step = pl.program_id(0)
    last = pl.num_programs(0) - 1
    width = cot_scr.shape[1]
    order = channel_minor()

    def put(row_block, source):
        rows = source[...].reshape(LANES, width)
        moved = jnp.dot(order, rows, preferred_element_type=F32)
        for tile_index in range(8):
            field[pl.ds(row_block * BH, BH), tile_index] = moved[
                :, tile_index * LANES : (tile_index + 1) * LANES
            ].reshape(BH, 8, LANES)

    @pl.when(step == 0)
    def _():
        put(0, top_ref)
        put(1, mid_ref)

    @pl.when(step == last)
    def _():
        put(step + 2, bot_ref)

    @pl.when(step < last)
    def _():
        put(step + 2, next_ref)

    rows = cot_ref[...].reshape(LANES, width)
    cot_scr[...] = jnp.dot(order, rows, preferred_element_type=F32).astype(BF16)
    for block in range(4):
        py = BH // 2 * offs[0, block, step] + srow[block, step]
        tile = offs[1, block, step]
        shift = scol[block, step]
        row_frac, col_frac = splat(fracs[0, block, step]), splat(fracs[1, block, step])
        both = jnp.concatenate(
            [
                col_taps(weights(col_frac), shift),
                col_taps(slopes(col_frac), shift),
            ],
            axis=1,
        )
        halves = jnp.concatenate(
            [
                cot_scr[:, block * BW : block * BW + LANES],
                cot_scr[:, block * BW + LANES : (block + 1) * BW],
            ],
            axis=0,
        )
        z_scr[block] = jnp.dot(halves, both, preferred_element_type=F32)
        by_value = [jnp.zeros((8, LANES), F32) for tap in range(4)]
        by_slope = [jnp.zeros((8, LANES), F32) for tap in range(4)]
        for part in range(3):
            pair = []
            for lane in (0, 2 * LANES):
                if part == 0:
                    z = z_scr[block, 0:LANES, lane : lane + LANES]
                elif part == 1:
                    z = (
                        z_scr[block, 0:LANES, lane + LANES : lane + 2 * LANES]
                        + z_scr[block, LANES:, lane : lane + LANES]
                    )
                else:
                    z = z_scr[block, LANES:, lane + LANES : lane + 2 * LANES]
                pair.append(z.reshape(BH, 8, LANES))
            source = (2 * block + 6 + part + tile) & 7
            for j in range(BH + 3):
                value = field[step * BH + py + j, source]
                for tap in range(4):
                    if 0 <= j - tap < BH:
                        by_value[tap] = by_value[tap] + value * pair[0][j - tap]
                        by_slope[tap] = by_slope[tap] + value * pair[1][j - tap]
        first = jnp.zeros((8, LANES), F32)
        second = jnp.zeros((8, LANES), F32)
        wy, sy = weights(row_frac), slopes(row_frac)
        for tap in range(4):
            first = first + sy[tap].astype(BF16).astype(F32) * by_value[tap]
            second = second + wy[tap].astype(BF16).astype(F32) * by_slope[tap]
        out_ref[0, block] = first
        out_ref[1, block] = second


def frac_sums(places, top, field, bottom, cot):
    channels, band_rows, columns = cot.shape
    blocks = band_rows // BH
    shape = (channels, BH, columns)
    return pl.pallas_call(
        frac_body,
        name="frac_sums",
        out_shape=jax.ShapeDtypeStruct((2, blocks * 4, 8, LANES), F32),
        grid_spec=pltpu.PrefetchScalarGridSpec(
            num_scalar_prefetch=4,
            grid=(blocks,),
            in_specs=[
                pl.BlockSpec(shape, lambda g, *a: (1, 0, 0)),
                pl.BlockSpec(shape, lambda g, *a: (0, 0, 0)),
                pl.BlockSpec(shape, lambda g, *a: (0, jnp.minimum(g + 1, blocks - 1), 0)),
                pl.BlockSpec(shape, lambda g, *a: (1, 0, 0)),
                pl.BlockSpec(shape, lambda g, *a: (0, g, 0)),
            ],
            out_specs=pl.BlockSpec((2, 4, 8, LANES), lambda g, *a: (0, g, 0, 0)),
            scratch_shapes=[
                pltpu.VMEM((BH * channels, columns), BF16),
                pltpu.VMEM((4, 2 * LANES, 4 * LANES), F32),
                pltpu.VMEM(((blocks + 2) * BH, columns // LANES, channels, LANES), F32),
            ],
        ),
        compiler_params=pltpu.CompilerParams(dimension_semantics=("arbitrary",)),
    )(*places, top, field, field, bottom, cot)


def gate_body(x_ref, w_in_t, half_bias, act_ref, slope_ref):
    part = 256
    for at in range(0, x_ref.shape[2], part):
        x = x_ref[0, :, at : at + part]
        half = jnp.dot(w_in_t[...], x, preferred_element_type=F32) + half_bias[...]
        twice = 1.0 + jnp.tanh(half)
        act = half * twice
        act_ref[0, :, at : at + part] = act.astype(BF16)
        slope_ref[0, :, at : at + part] = (twice + act * (2.0 - twice)).astype(BF16)


def gate(x, w_in, bias):
    rows, channels, columns = x.shape
    whole = lambda shape: pl.BlockSpec(shape, lambda r: (0,) * len(shape))
    tile = lambda height: pl.BlockSpec((1, height, columns), lambda r: (r, 0, 0))
    half = jnp.asarray(0.5, BF16)
    return pl.pallas_call(
        gate_body,
        name="gate",
        out_shape=(jax.ShapeDtypeStruct((rows, HID, columns), BF16),) * 2,
        grid=(rows,),
        in_specs=[tile(channels), whole((HID, channels)), whole((HID, 1))],
        out_specs=[tile(HID), tile(HID)],
        compiler_params=pltpu.CompilerParams(dimension_semantics=("arbitrary",)),
    )(x, w_in.T * half, 0.5 * bias[:, None])


def mlp_body(
    x_ref, dy_ref, act_ref, slope_ref, w_in, w_out, tail_ref, dx_ref, send_ref, g_in, g_out, g_bias,
    dpre_scr
):
    row = pl.program_id(0)

    @pl.when(row == 0)
    def _():
        g_in[...] = jnp.zeros_like(g_in)
        g_out[...] = jnp.zeros_like(g_out)
        g_bias[...] = jnp.zeros_like(g_bias)

    part = 256
    points = (((1,), (1,)), ((), ()))

    def gates(at):
        dy = dy_ref[:, :, at : at + part].reshape(C, part)
        dact = jnp.dot(w_out[...], dy, preferred_element_type=F32)
        dpre = (dact * slope_ref[0, :, at : at + part].astype(F32)).astype(BF16)
        dpre_scr[:, at : at + part] = dpre
        total = g_bias[...]
        for lane in range(0, part, LANES):
            total = total + dpre[:, lane : lane + LANES].astype(F32)
        g_bias[...] = total

    def products(at):
        x = x_ref[0, :, at : at + part]
        dy = dy_ref[:, :, at : at + part].reshape(C, part)
        dpre = dpre_scr[:, at : at + part]
        dx = dy.astype(F32) + jnp.dot(w_in[...], dpre, preferred_element_type=F32)
        dx_ref[0, :, at : at + part] = dx.astype(BF16)
        g_in[...] += lax.dot_general(dpre, x, points, preferred_element_type=F32)
        g_out[...] += lax.dot_general(
            act_ref[0, :, at : at + part], dy, points, preferred_element_type=F32
        )

    width = x_ref.shape[2]
    gates(0)
    for at in range(part, width, part):
        gates(at)
        products(at - part)
    products(width - part)

    @pl.when(row == pl.num_programs(0) - 1)
    def _():
        parts, each, lanes = send_ref.shape
        shift = jnp.sum(g_bias[...], axis=1, keepdims=True)
        high = shift.astype(BF16).astype(F32)
        lane = lax.broadcasted_iota(jnp.int32, (HID, LANES), 1)
        tail = jnp.where(lane == 0, high, jnp.where(lane == 1, shift - high, tail_ref[...]))
        send = jnp.concatenate([g_in[...], g_out[...], tail], axis=1)
        send_ref[...] = send.reshape(parts, each, lanes).astype(BF16)


def mlp(x, dy, act, slope, w_in, w_out, tail, parts):
    rows, channels, columns = x.shape
    sources = dy.shape[0]
    whole = lambda shape: pl.BlockSpec(shape, lambda r: (0,) * len(shape))
    tile = lambda height: pl.BlockSpec((1, height, columns), lambda r: (r, 0, 0))
    send = (parts, HID // parts, 2 * channels + LANES)
    return pl.pallas_call(
        mlp_body,
        name="mlp",
        out_shape=(
            jax.ShapeDtypeStruct((rows, channels, columns), BF16),
            jax.ShapeDtypeStruct(send, BF16),
        ),
        grid=(rows,),
        in_specs=[
            tile(channels),
            pl.BlockSpec((sources, None, 8, columns), lambda r: (0, r, 0, 0)),
            tile(HID),
            tile(HID),
            whole((channels, HID)),
            whole((HID, channels)),
            whole((HID, LANES)),
        ],
        out_specs=[tile(channels), whole(send)],
        scratch_shapes=[
            pltpu.VMEM((HID, channels), F32),
            pltpu.VMEM((HID, channels), F32),
            pltpu.VMEM((HID, LANES), F32),
            pltpu.VMEM((HID, columns), BF16),
        ],
        compiler_params=pltpu.CompilerParams(dimension_semantics=("arbitrary",)),
    )(x, dy, act, slope, w_in, w_out * jnp.asarray(0.5, BF16), tail)


def finish_body(scale, frac_scale, got_ref, first_ref, second_ref, shift_ref, frac_ref):
    total = got_ref[...]
    each = total.shape[0]
    held = 2 * frac_ref.shape[2]
    first_ref[...] = total[:, 0:C] * scale
    second_ref[...] = total[:, C : 2 * C] * scale
    tail = total[:, 2 * C :]
    lane = lax.broadcasted_iota(jnp.int32, (each, LANES), 1)
    row = lax.broadcasted_iota(jnp.int32, (each, LANES), 0)
    shift = tail[:, 0:1] + tail[:, 1:2]
    shift = jnp.sum(jnp.where(lane == row, shift, 0.0), axis=0, keepdims=True)
    shift_ref[...] = shift[:, 0:each] * scale
    frac = tail[:, held : 2 * held] + tail[:, 2 * held : 3 * held]
    half = held // 2
    frac_ref[0] = frac[:, 0:half] * frac_scale
    frac_ref[1] = frac[:, half:] * frac_scale


def finish(got, scale, frac_scale, row_blocks):
    each = got.shape[0]
    return pl.pallas_call(
        functools.partial(finish_body, scale, frac_scale),
        name="finish",
        out_shape=(
            jax.ShapeDtypeStruct((each, C), F32),
            jax.ShapeDtypeStruct((each, C), F32),
            jax.ShapeDtypeStruct((1, each), F32),
            jax.ShapeDtypeStruct((2, each, row_blocks), F32),
        ),
        in_specs=[pl.BlockSpec(memory_space=pltpu.VMEM)],
    )(got)


def shards(
    inputs, w_in, bias_in, w_out, advected, cotangent, offsets, stencil_row, stencil_col, fracs
):
    channels_dev, band_rows, columns = advected.shape
    row_blocks = band_rows // BH
    point_rows = inputs.shape[1]
    lat = lax.axis_size("lat")
    grp = lax.axis_size("grp")

    places = (
        offsets.transpose(0, 2, 1),
        stencil_row.T,
        stencil_col.T,
        fracs.transpose(0, 2, 1),
    )
    head, tail = pack(places, cotangent, advected)
    top, bottom = exchange(head, tail)
    dy_band, edges = spread(places, cotangent)
    meta = jnp.stack([halo[2 * channels_dev, 0, : 3 * LANES] for halo in (top, bottom)])
    dy_band = spread_edges(meta.astype(F32), top, bottom, edges, dy_band)
    dy_send = dy_band.reshape(grp, point_rows, channels_dev, columns)
    dy_points = lax.all_to_all(dy_send, "grp", split_axis=0, concat_axis=0, tiled=True)

    frac_parts = frac_sums(places, top, advected, bottom, cotangent)
    parts = lat * grp
    each = HID // parts
    held = 2 * row_blocks
    frac_local = jnp.sum(frac_parts, axis=(2, 3)).reshape(held, columns // BW).T
    high = lax.reduce_precision(frac_local, 8, 7)
    both = jnp.stack([high, frac_local - high], axis=1)
    mine = jnp.where(jnp.arange(lat) == lax.axis_index("lat"), 1.0, 0.0)
    slots = mine[:, None, None, None] * both.reshape(1, 1, each, 2 * held)
    slots = jnp.broadcast_to(slots, (lat, grp, each, 2 * held)).reshape(HID, 2 * held)
    extra = jnp.pad(slots, ((0, 0), (held, LANES - 3 * held)))

    x_rows = inputs.transpose(1, 0, 2)
    act, slope = gate(x_rows, w_in, bias_in)
    dx_rows, send = mlp(x_rows, dy_points, act, slope, w_in, w_out, extra, parts)
    grad_inputs = dx_rows.transpose(1, 0, 2)

    got = lax.all_to_all(send, ("lat", "grp"), split_axis=0, concat_axis=0, tiled=True)
    scale = 1.0 / math.sqrt(point_rows * columns * parts)
    first, second, shift, frac = finish(jnp.sum(got.astype(F32), axis=0), scale, 1.0 / math.sqrt(C * BH * BW), row_blocks)
    return (grad_inputs, first.T, shift.reshape(each), second, frac.transpose(0, 2, 1))


def solution(mesh):
    placed = (
        P(None, ("lat", "grp"), None),
        P(),
        P(),
        P(),
        P("grp", "lat", None),
        P("grp", "lat", None),
        P(None, "lat", None),
        P("lat", None),
        P("lat", None),
        P(None, "lat", None),
    )
    return jax.shard_map(
        shards,
        mesh=mesh,
        in_specs=placed,
        out_specs=(
            P(None, ("lat", "grp"), None),
            P(None, ("lat", "grp")),
            P(("lat", "grp")),
            P(("lat", "grp"), None),
            P(None, "lat", None),
        ),
        check_vma=False,
    )
```

```python
import functools
import math

import jax
import jax.numpy as jnp
from jax import lax
from jax.experimental import pallas as pl
from jax.experimental.pallas import tpu as pltpu
from jax.sharding import PartitionSpec as P

C = 256
BH = 16
BW = 256
LANES = 128
HID = 512
F32 = jnp.float32
BF16 = jnp.bfloat16


EDGE = 5


def weights(frac):
    square = frac * frac
    cube = square * frac
    return (
        0.5 * (-cube + 2.0 * square - frac),
        0.5 * (3.0 * cube - 5.0 * square + 2.0),
        0.5 * (-3.0 * cube + 4.0 * square + frac),
        0.5 * (cube - square),
    )


def slopes(frac):
    square = frac * frac
    return (
        0.5 * (-3.0 * square + 4.0 * frac - 1.0),
        0.5 * (9.0 * square - 10.0 * frac),
        0.5 * (-9.0 * square + 8.0 * frac + 1.0),
        0.5 * (3.0 * square - 2.0 * frac),
    )


def splat(value):
    return jnp.full((8, LANES), value, F32)


def exchange(head, tail):
    count = lax.axis_size("lat")
    above = lax.ppermute(tail, "lat", [(i, i + 1) for i in range(count - 1)])
    below = lax.ppermute(head, "lat", [(i + 1, i) for i in range(count - 1)])
    return above, below


def channel_minor():
    out = lax.broadcasted_iota(jnp.int32, (LANES, LANES), 0)
    src = lax.broadcasted_iota(jnp.int32, (LANES, LANES), 1)
    return ((out % 8) * 16 + out // 8 == src).astype(F32).astype(BF16)


def lanes():
    lane = lax.broadcasted_iota(jnp.int32, (8, LANES), 1)
    return lane, lax.broadcasted_iota(jnp.int32, (8, LANES), 0)


def col_taps(values, shift):
    lane, row = lanes()
    base = jnp.zeros((8, LANES), F32)
    for tap in range(4):
        base = jnp.where(lane - row == tap, values[tap], base)
    left, right = [], []
    for group in range(0, LANES, 8):
        moved = pltpu.roll(base, (shift + group) & (LANES - 1), 1)
        inside = lane - row >= shift + group
        left.append(jnp.where(inside, moved, 0.0))
        right.append(jnp.where(inside, 0.0, moved))
    both = [jnp.concatenate(left, axis=0), jnp.concatenate(right, axis=0)]
    return jnp.concatenate(both, axis=1).astype(BF16)


REACH = BH + 4


def row_taps(values):
    lane, row = lanes()
    base = jnp.zeros((8, LANES), F32)
    for tap in range(4):
        base = jnp.where((lane - BH * row + tap) & (LANES - 1) == 0, values[tap], base)
    own = lane // BH == row
    moved = [base] + [pltpu.roll(base, step, 1) for step in range(1, REACH)]
    return jnp.concatenate([jnp.where(own, part, 0.0) for part in moved], axis=0).astype(BF16)


def pack_body(offs, srow, scol, fracs, cot, adv, head_ref, tail_ref, rows, meta, arrived, left):
    channels = cot.shape[0]
    last = offs.shape[2] - 1
    inward, outward = [], []
    for side, (out_ref, row) in enumerate(((head_ref, 0), (tail_ref, last))):
        for which, source in enumerate((cot, adv)):
            job = 2 * side + which
            inward.append(
                pltpu.make_async_copy(
                    source.at[:, row * BH : (row + 1) * BH, :], rows.at[job], arrived.at[job]
                )
            )
            place = slice(which * channels, (which + 1) * channels)
            outward.append(
                pltpu.make_async_copy(rows.at[job], out_ref.at[place], left.at[job])
            )
    for job in inward:
        job.start()
    lane = lax.broadcasted_iota(jnp.int32, (BH, LANES), 1)
    for side, (out_ref, row) in enumerate(((head_ref, 0), (tail_ref, last))):
        value = jnp.zeros((BH, LANES), F32)
        for block in range(4):
            own = [
                (BH // 2 * offs[0, block, row] + srow[block, row]).astype(F32),
                offs[1, block, row].astype(F32),
                scol[block, row].astype(F32),
                fracs[0, block, row],
                fracs[1, block, row],
            ]
            for slot, entry in enumerate(own):
                value = jnp.where(lane == block * EDGE + slot, entry, value)
        meta[side] = jnp.zeros(meta.shape[1:], BF16)
        for part in range(3):
            high = value.astype(BF16)
            meta[side, :, part * LANES : (part + 1) * LANES] = high
            value = value - high.astype(F32)
        outward.append(
            pltpu.make_async_copy(meta.at[side], out_ref.at[2 * channels], left.at[4 + side])
        )
        outward[-1].start()
    for job in range(4):
        inward[job].wait()
        outward[job].start()
    for job in outward:
        job.wait()


def pack(places, cot, adv):
    channels, band_rows, columns = cot.shape
    shape = jax.ShapeDtypeStruct((2 * channels + 1, BH, columns), BF16)
    anywhere = pl.BlockSpec(memory_space=pl.ANY)
    return pl.pallas_call(
        pack_body,
        name="pack",
        out_shape=(shape, shape),
        grid_spec=pltpu.PrefetchScalarGridSpec(
            num_scalar_prefetch=4,
            grid=(1,),
            in_specs=[anywhere, anywhere],
            out_specs=[anywhere, anywhere],
            scratch_shapes=[
                pltpu.VMEM((4, channels, BH, columns), BF16),
                pltpu.VMEM((2, BH, columns), BF16),
                pltpu.SemaphoreType.DMA((4,)),
                pltpu.SemaphoreType.DMA((6,)),
            ],
        ),
        compiler_params=pltpu.CompilerParams(dimension_semantics=("arbitrary",)),
    )(*places, cot, adv)


def spread_blocks(jobs, tap_scr, row_scr, z_scr, acc):
    for job, (rows, block, first, py, tile, shift, wx, wy) in enumerate(jobs):
        tap_scr[job] = col_taps(wx, shift)
        row_scr[job] = row_taps(wy)
    for job, (rows, block, first, py, tile, shift, wx, wy) in enumerate(jobs):
        z = jnp.dot(halves_of(rows, block), tap_scr[job], preferred_element_type=F32)
        z_scr[job, :, 0:LANES] = z[0:LANES, 0:LANES].astype(BF16)
        middle = z[0:LANES, LANES:] + z[LANES:, 0:LANES]
        z_scr[job, :, LANES : 2 * LANES] = middle.astype(BF16)
        z_scr[job, :, 2 * LANES :] = z[LANES:, LANES:].astype(BF16)
    moved = [
        jnp.dot(row_scr[job], z_scr[job], preferred_element_type=F32) for job in range(len(jobs))
    ]
    for job, (rows, block, first, py, tile, shift, wx, wy) in enumerate(jobs):
        for part in range(3):
            target = (2 * block + 6 + part + tile) & 7
            value = moved[job][:, part * LANES : (part + 1) * LANES].reshape(REACH, 8, LANES)
            at = pl.ds(first + py, REACH)
            acc[at, target] = acc[at, target] + value


def spread_scratch():
    return [
        pltpu.VMEM((8, LANES, 2 * LANES), BF16),
        pltpu.VMEM((8, REACH * 8, LANES), BF16),
        pltpu.VMEM((8, LANES, 3 * LANES), BF16),
    ]


def halves_of(rows, block):
    return jnp.concatenate(
        [
            rows[:, block * BW : block * BW + LANES],
            rows[:, block * BW + LANES : (block + 1) * BW],
        ],
        axis=0,
    )


def emit(acc, first, out_ref):
    for tile_index in range(8):
        done = acc[pl.ds(first, BH), tile_index].reshape(BH * 8, LANES)
        out_ref[:, tile_index * LANES : (tile_index + 1) * LANES] = done.astype(BF16)


def spread_body(offs, srow, scol, fracs, cot_ref, out_ref, edge_ref, tap_scr, row_scr, z_scr, acc):
    step = pl.program_id(0)
    last = pl.num_programs(0) - 1

    @pl.when(step == 0)
    def _():
        acc[0 : 2 * BH] = jnp.zeros((2 * BH,) + acc.shape[1:], F32)

    @pl.when(step < last)
    def _():
        acc[pl.ds((2 * step + 2) * BH, 2 * BH)] = jnp.zeros((2 * BH,) + acc.shape[1:], F32)
        jobs = []
        for half in range(2):
            row = 2 * step + half
            rows = cot_ref[:, half * BH : (half + 1) * BH].reshape(LANES, cot_ref.shape[2])
            for block in range(4):
                jobs.append(
                    (
                        rows,
                        block,
                        row * BH,
                        BH // 2 * offs[0, block, row] + srow[block, row],
                        offs[1, block, row],
                        scol[block, row],
                        weights(splat(fracs[1, block, row])),
                        weights(splat(fracs[0, block, row])),
                    )
                )
        spread_blocks(jobs, tap_scr, row_scr, z_scr, acc)

    emit(acc, jnp.maximum(2 * step - 1, 0) * BH, out_ref.at[0])
    emit(acc, 2 * step * BH, out_ref.at[1])

    @pl.when(step == 0)
    def _():
        edge_ref[0] = acc[BH : 2 * BH]

    @pl.when(step == last)
    def _():
        edge_ref[0] = acc[pl.ds(2 * last * BH, BH)]


def spread(places, cot):
    channels, band_rows, columns = cot.shape
    blocks = band_rows // BH
    pairs = blocks // 2
    tiles = columns // LANES
    return pl.pallas_call(
        spread_body,
        name="spread",
        out_shape=(
            jax.ShapeDtypeStruct((blocks, BH * channels, columns), BF16),
            jax.ShapeDtypeStruct((2, BH, tiles, channels, LANES), F32),
        ),
        grid_spec=pltpu.PrefetchScalarGridSpec(
            num_scalar_prefetch=4,
            grid=(pairs + 1,),
            in_specs=[
                pl.BlockSpec(
                    (channels, 2 * BH, columns), lambda g, *a: (0, jnp.minimum(g, pairs - 1), 0)
                )
            ],
            out_specs=[
                pl.BlockSpec(
                    (2, BH * channels, columns), lambda g, *a: (jnp.maximum(g - 1, 0), 0, 0)
                ),
                pl.BlockSpec(
                    (1, BH, tiles, channels, LANES),
                    lambda g, *a: (jnp.where(g == pairs, 1, 0), 0, 0, 0, 0),
                ),
            ],
            scratch_shapes=spread_scratch()
            + [pltpu.VMEM(((blocks + 2) * BH, tiles, channels, LANES), F32)],
        ),
        compiler_params=pltpu.CompilerParams(dimension_semantics=("arbitrary",)),
    )(*places, cot)


def edge_body(meta, top_ref, bot_ref, edge_ref, whole, out_ref, tap_scr, row_scr, z_scr, acc):
    step = pl.program_id(0)
    upper, lower = 2 * BH, 3 * BH

    @pl.when(step == 0)
    def _():
        acc[0:upper] = jnp.zeros((upper,) + acc.shape[1:], F32)
        acc[upper : upper + BH] = edge_ref[0]
        acc[lower : lower + BH] = edge_ref[1]
        acc[lower + BH :] = jnp.zeros((2 * BH,) + acc.shape[1:], F32)
        jobs = []
        for side, ref in enumerate((top_ref, bot_ref)):
            rows = ref[0 : LANES // BH].reshape(LANES, ref.shape[2])
            for block in range(4):
                at = [block * EDGE + slot for slot in range(EDGE)]
                place = [meta[side, k].astype(jnp.int32) for k in at[:3]]
                fracs = [
                    meta[side, k] + meta[side, LANES + k] + meta[side, 2 * LANES + k]
                    for k in at[3:]
                ]
                wy, wx = [weights(splat(frac)) for frac in fracs]
                jobs.append((rows, block, side * lower, *place, wx, wy))
        spread_blocks(jobs, tap_scr, row_scr, z_scr, acc)

    emit(acc, upper + step * BH, out_ref.at[0])


def spread_edges(meta, top, bottom, edges, dy):
    blocks, rows, columns = dy.shape
    channels = edges.shape[3]
    return pl.pallas_call(
        edge_body,
        name="spread_edges",
        out_shape=jax.ShapeDtypeStruct(dy.shape, dy.dtype),
        grid_spec=pltpu.PrefetchScalarGridSpec(
            num_scalar_prefetch=1,
            grid=(2,),
            in_specs=[
                pl.BlockSpec((channels, BH, columns), lambda g, a: (0, 0, 0)),
                pl.BlockSpec((channels, BH, columns), lambda g, a: (0, 0, 0)),
                pl.BlockSpec(edges.shape, lambda g, a: (0, 0, 0, 0, 0)),
                pl.BlockSpec(memory_space=pl.ANY),
            ],
            out_specs=pl.BlockSpec((1, rows, columns), lambda g, a: (g * (blocks - 1), 0, 0)),
            scratch_shapes=spread_scratch() + [pltpu.VMEM((6 * BH,) + edges.shape[2:], F32)],
        ),
        input_output_aliases={4: 0},
        compiler_params=pltpu.CompilerParams(dimension_semantics=("arbitrary",)),
    )(meta, top, bottom, edges, dy)


def frac_body(
    offs, srow, scol, fracs, top_ref, mid_ref, next_ref, bot_ref, cot_ref, out_ref, cot_scr, z_scr, field
):
    step = pl.program_id(0)
    last = pl.num_programs(0) - 1
    width = cot_scr.shape[1]
    order = channel_minor()

    def put(row_block, source):
        rows = source[...].reshape(LANES, width)
        moved = jnp.dot(order, rows, preferred_element_type=F32)
        for tile_index in range(8):
            field[pl.ds(row_block * BH, BH), tile_index] = moved[
                :, tile_index * LANES : (tile_index + 1) * LANES
            ].reshape(BH, 8, LANES)

    @pl.when(step == 0)
    def _():
        put(0, top_ref)
        put(1, mid_ref)

    @pl.when(step == last)
    def _():
        put(step + 2, bot_ref)

    @pl.when(step < last)
    def _():
        put(step + 2, next_ref)

    rows = cot_ref[...].reshape(LANES, width)
    cot_scr[...] = jnp.dot(order, rows, preferred_element_type=F32).astype(BF16)
    for block in range(4):
        py = BH // 2 * offs[0, block, step] + srow[block, step]
        tile = offs[1, block, step]
        shift = scol[block, step]
        row_frac, col_frac = splat(fracs[0, block, step]), splat(fracs[1, block, step])
        both = jnp.concatenate(
            [
                col_taps(weights(col_frac), shift),
                col_taps(slopes(col_frac), shift),
            ],
            axis=1,
        )
        halves = jnp.concatenate(
            [
                cot_scr[:, block * BW : block * BW + LANES],
                cot_scr[:, block * BW + LANES : (block + 1) * BW],
            ],
            axis=0,
        )
        z_scr[block] = jnp.dot(halves, both, preferred_element_type=F32)
        by_value = [jnp.zeros((8, LANES), F32) for tap in range(4)]
        by_slope = [jnp.zeros((8, LANES), F32) for tap in range(4)]
        for part in range(3):
            pair = []
            for lane in (0, 2 * LANES):
                if part == 0:
                    z = z_scr[block, 0:LANES, lane : lane + LANES]
                elif part == 1:
                    z = (
                        z_scr[block, 0:LANES, lane + LANES : lane + 2 * LANES]
                        + z_scr[block, LANES:, lane : lane + LANES]
                    )
                else:
                    z = z_scr[block, LANES:, lane + LANES : lane + 2 * LANES]
                pair.append(z.reshape(BH, 8, LANES))
            source = (2 * block + 6 + part + tile) & 7
            for j in range(BH + 3):
                value = field[step * BH + py + j, source]
                for tap in range(4):
                    if 0 <= j - tap < BH:
                        by_value[tap] = by_value[tap] + value * pair[0][j - tap]
                        by_slope[tap] = by_slope[tap] + value * pair[1][j - tap]
        first = jnp.zeros((8, LANES), F32)
        second = jnp.zeros((8, LANES), F32)
        wy, sy = weights(row_frac), slopes(row_frac)
        for tap in range(4):
            first = first + sy[tap].astype(BF16).astype(F32) * by_value[tap]
            second = second + wy[tap].astype(BF16).astype(F32) * by_slope[tap]
        out_ref[0, block] = first
        out_ref[1, block] = second


def frac_sums(places, top, field, bottom, cot):
    channels, band_rows, columns = cot.shape
    blocks = band_rows // BH
    shape = (channels, BH, columns)
    return pl.pallas_call(
        frac_body,
        name="frac_sums",
        out_shape=jax.ShapeDtypeStruct((2, blocks * 4, 8, LANES), F32),
        grid_spec=pltpu.PrefetchScalarGridSpec(
            num_scalar_prefetch=4,
            grid=(blocks,),
            in_specs=[
                pl.BlockSpec(shape, lambda g, *a: (1, 0, 0)),
                pl.BlockSpec(shape, lambda g, *a: (0, 0, 0)),
                pl.BlockSpec(shape, lambda g, *a: (0, jnp.minimum(g + 1, blocks - 1), 0)),
                pl.BlockSpec(shape, lambda g, *a: (1, 0, 0)),
                pl.BlockSpec(shape, lambda g, *a: (0, g, 0)),
            ],
            out_specs=pl.BlockSpec((2, 4, 8, LANES), lambda g, *a: (0, g, 0, 0)),
            scratch_shapes=[
                pltpu.VMEM((BH * channels, columns), BF16),
                pltpu.VMEM((4, 2 * LANES, 4 * LANES), F32),
                pltpu.VMEM(((blocks + 2) * BH, columns // LANES, channels, LANES), F32),
            ],
        ),
        compiler_params=pltpu.CompilerParams(dimension_semantics=("arbitrary",)),
    )(*places, top, field, field, bottom, cot)


def gate_body(x_ref, w_in_t, half_bias, act_ref, slope_ref):
    part = 256
    for at in range(0, x_ref.shape[2], part):
        x = x_ref[0, :, at : at + part]
        half = jnp.dot(w_in_t[...], x, preferred_element_type=F32) + half_bias[...]
        twice = 1.0 + jnp.tanh(half)
        act = half * twice
        act_ref[0, :, at : at + part] = act.astype(BF16)
        slope_ref[0, :, at : at + part] = (twice + act * (2.0 - twice)).astype(BF16)


def gate(x, half_w_in_t, half_bias):
    rows, channels, columns = x.shape
    rows = rows // 2
    whole = lambda shape: pl.BlockSpec(shape, lambda r: (0,) * len(shape))
    tile = lambda height: pl.BlockSpec((1, height, columns), lambda r: (r, 0, 0))
    return pl.pallas_call(
        gate_body,
        name="gate",
        out_shape=(jax.ShapeDtypeStruct((rows, HID, columns), BF16),) * 2,
        grid=(rows,),
        in_specs=[
            pl.BlockSpec((1, channels, columns), lambda r: (2 * r + 1, 0, 0)),
            whole((HID, channels)),
            whole((HID, 1)),
        ],
        out_specs=[tile(HID), tile(HID)],
        compiler_params=pltpu.CompilerParams(dimension_semantics=("arbitrary",)),
    )(x, half_w_in_t, half_bias)


def mlp_body(
    x_ref, dy_ref, act_ref, slope_ref, w_in_t, half_bias, w_in, w_out, tail_ref, dx_ref, send_ref,
    g_in, g_out, g_bias, act_scr, dpre_scr
):
    step = pl.program_id(0)

    @pl.when(step == 0)
    def _():
        g_in[...] = jnp.zeros_like(g_in)
        g_out[...] = jnp.zeros_like(g_out)
        g_bias[...] = jnp.zeros_like(g_bias)

    part = 256
    points = (((1,), (1,)), ((), ()))

    def field(item):
        row, cut = item
        return dy_ref[:, row, :, cut].reshape(C, part)

    def gates(item, slot):
        row, cut = item
        if row == 0:
            half = jnp.dot(w_in_t[...], x_ref[0, :, cut], preferred_element_type=F32)
            half = half + half_bias[...]
            twice = 1.0 + jnp.tanh(half)
            act = half * twice
            act_scr[slot] = act.astype(BF16)
            slope = twice + act * (2.0 - twice)
        else:
            slope = slope_ref[0, :, cut].astype(F32)
        dact = jnp.dot(w_out[...], field(item), preferred_element_type=F32)
        dpre = (dact * slope).astype(BF16)
        dpre_scr[slot] = dpre
        total = g_bias[...]
        for lane in range(0, part, LANES):
            total = total + dpre[:, lane : lane + LANES].astype(F32)
        g_bias[...] = total

    def products(item, slot):
        row, cut = item
        dy = field(item)
        dpre = dpre_scr[slot]
        dx = dy.astype(F32) + jnp.dot(w_in[...], dpre, preferred_element_type=F32)
        dx_ref[row, :, cut] = dx.astype(BF16)
        g_in[...] += lax.dot_general(dpre, x_ref[row, :, cut], points, preferred_element_type=F32)
        act = act_scr[slot] if row == 0 else act_ref[0, :, cut]
        g_out[...] += lax.dot_general(act, dy, points, preferred_element_type=F32)

    items = []
    for at in range(0, x_ref.shape[2], part):
        items.extend([(0, slice(at, at + part)), (1, slice(at, at + part))])
    gates(items[0], 0)
    for index in range(1, len(items)):
        gates(items[index], index % 3)
        products(items[index - 1], (index - 1) % 3)
    products(items[-1], (len(items) - 1) % 3)

    @pl.when(step == pl.num_programs(0) - 1)
    def _():
        parts, each, lanes = send_ref.shape
        shift = jnp.sum(g_bias[...], axis=1, keepdims=True)
        high = shift.astype(BF16).astype(F32)
        lane = lax.broadcasted_iota(jnp.int32, (HID, LANES), 1)
        tail = jnp.where(lane == 0, high, jnp.where(lane == 1, shift - high, tail_ref[...]))
        send = jnp.concatenate([g_in[...], g_out[...], tail], axis=1)
        send_ref[...] = send.reshape(parts, each, lanes).astype(BF16)


def mlp(x, dy, act, slope, half_w_in_t, half_bias, w_in, w_out, tail, parts):
    rows, channels, columns = x.shape
    sources = dy.shape[0]
    whole = lambda shape: pl.BlockSpec(shape, lambda r: (0,) * len(shape))
    pair = pl.BlockSpec((2, channels, columns), lambda r: (r, 0, 0))
    ready = pl.BlockSpec((1, HID, columns), lambda r: (r, 0, 0))
    send = (parts, HID // parts, 2 * channels + LANES)
    return pl.pallas_call(
        mlp_body,
        name="mlp",
        out_shape=(
            jax.ShapeDtypeStruct((rows, channels, columns), BF16),
            jax.ShapeDtypeStruct(send, BF16),
        ),
        grid=(rows // 2,),
        in_specs=[
            pair,
            pl.BlockSpec((sources, 2, 8, columns), lambda r: (0, r, 0, 0)),
            ready,
            ready,
            whole((HID, channels)),
            whole((HID, 1)),
            whole((channels, HID)),
            whole((HID, channels)),
            whole((HID, LANES)),
        ],
        out_specs=[pair, whole(send)],
        scratch_shapes=[
            pltpu.VMEM((HID, channels), F32),
            pltpu.VMEM((HID, channels), F32),
            pltpu.VMEM((HID, LANES), F32),
            pltpu.VMEM((3, HID, 256), BF16),
            pltpu.VMEM((3, HID, 256), BF16),
        ],
        compiler_params=pltpu.CompilerParams(dimension_semantics=("arbitrary",)),
    )(x, dy, act, slope, half_w_in_t, half_bias, w_in, w_out * jnp.asarray(0.5, BF16), tail)


def finish_body(scale, frac_scale, got_ref, first_ref, second_ref, shift_ref, frac_ref):
    total = got_ref[...]
    each = total.shape[0]
    held = 2 * frac_ref.shape[2]
    first_ref[...] = total[:, 0:C] * scale
    second_ref[...] = total[:, C : 2 * C] * scale
    tail = total[:, 2 * C :]
    lane = lax.broadcasted_iota(jnp.int32, (each, LANES), 1)
    row = lax.broadcasted_iota(jnp.int32, (each, LANES), 0)
    shift = tail[:, 0:1] + tail[:, 1:2]
    shift = jnp.sum(jnp.where(lane == row, shift, 0.0), axis=0, keepdims=True)
    shift_ref[...] = shift[:, 0:each] * scale
    frac = tail[:, held : 2 * held] + tail[:, 2 * held : 3 * held]
    half = held // 2
    frac_ref[0] = frac[:, 0:half] * frac_scale
    frac_ref[1] = frac[:, half:] * frac_scale


def finish(got, scale, frac_scale, row_blocks):
    each = got.shape[0]
    return pl.pallas_call(
        functools.partial(finish_body, scale, frac_scale),
        name="finish",
        out_shape=(
            jax.ShapeDtypeStruct((each, C), F32),
            jax.ShapeDtypeStruct((each, C), F32),
            jax.ShapeDtypeStruct((1, each), F32),
            jax.ShapeDtypeStruct((2, each, row_blocks), F32),
        ),
        in_specs=[pl.BlockSpec(memory_space=pltpu.VMEM)],
    )(got)


def shards(
    inputs, w_in, bias_in, w_out, advected, cotangent, offsets, stencil_row, stencil_col, fracs
):
    channels_dev, band_rows, columns = advected.shape
    row_blocks = band_rows // BH
    point_rows = inputs.shape[1]
    lat = lax.axis_size("lat")
    grp = lax.axis_size("grp")

    places = (
        offsets.transpose(0, 2, 1),
        stencil_row.T,
        stencil_col.T,
        fracs.transpose(0, 2, 1),
    )
    head, tail = pack(places, cotangent, advected)
    top, bottom = exchange(head, tail)
    dy_band, edges = spread(places, cotangent)
    meta = jnp.stack([halo[2 * channels_dev, 0, : 3 * LANES] for halo in (top, bottom)])
    dy_band = spread_edges(meta.astype(F32), top, bottom, edges, dy_band)
    dy_send = dy_band.reshape(grp, point_rows, channels_dev, columns)
    dy_points = lax.all_to_all(dy_send, "grp", split_axis=0, concat_axis=0, tiled=True)

    frac_parts = frac_sums(places, top, advected, bottom, cotangent)
    parts = lat * grp
    each = HID // parts
    held = 2 * row_blocks
    frac_local = jnp.sum(frac_parts, axis=(2, 3)).reshape(held, columns // BW).T
    high = lax.reduce_precision(frac_local, 8, 7)
    both = jnp.stack([high, frac_local - high], axis=1)
    mine = jnp.where(jnp.arange(lat) == lax.axis_index("lat"), 1.0, 0.0)
    slots = mine[:, None, None, None] * both.reshape(1, 1, each, 2 * held)
    slots = jnp.broadcast_to(slots, (lat, grp, each, 2 * held)).reshape(HID, 2 * held)
    extra = jnp.pad(slots, ((0, 0), (held, LANES - 3 * held)))

    x_rows = inputs.transpose(1, 0, 2)
    half_w_in_t = w_in.T * jnp.asarray(0.5, BF16)
    half_bias = 0.5 * bias_in[:, None]
    act, slope = gate(x_rows, half_w_in_t, half_bias)
    dx_rows, send = mlp(
        x_rows, dy_points, act, slope, half_w_in_t, half_bias, w_in, w_out, extra, parts
    )
    grad_inputs = dx_rows.transpose(1, 0, 2)

    got = lax.all_to_all(send, ("lat", "grp"), split_axis=0, concat_axis=0, tiled=True)
    scale = 1.0 / math.sqrt(point_rows * columns * parts)
    first, second, shift, frac = finish(jnp.sum(got.astype(F32), axis=0), scale, 1.0 / math.sqrt(C * BH * BW), row_blocks)
    return (grad_inputs, first.T, shift.reshape(each), second, frac.transpose(0, 2, 1))


def solution(mesh):
    placed = (
        P(None, ("lat", "grp"), None),
        P(),
        P(),
        P(),
        P("grp", "lat", None),
        P("grp", "lat", None),
        P(None, "lat", None),
        P("lat", None),
        P("lat", None),
        P(None, "lat", None),
    )
    return jax.shard_map(
        shards,
        mesh=mesh,
        in_specs=placed,
        out_specs=(
            P(None, ("lat", "grp"), None),
            P(None, ("lat", "grp")),
            P(("lat", "grp")),
            P(("lat", "grp"), None),
            P(None, "lat", None),
        ),
        check_vma=False,
    )
```

```python
import functools
import math

import jax
import jax.numpy as jnp
from jax import lax
from jax.experimental import pallas as pl
from jax.experimental.pallas import tpu as pltpu
from jax.sharding import PartitionSpec as P


C = 256
BH = 16
BW = 256
LANES = 128
HID = 512
F32 = jnp.float32
BF16 = jnp.bfloat16


EDGE = 5


def weights(frac):
    square = frac * frac
    cube = square * frac
    return (
        0.5 * (-cube + 2.0 * square - frac),
        0.5 * (3.0 * cube - 5.0 * square + 2.0),
        0.5 * (-3.0 * cube + 4.0 * square + frac),
        0.5 * (cube - square),
    )


def slopes(frac):
    square = frac * frac
    return (
        0.5 * (-3.0 * square + 4.0 * frac - 1.0),
        0.5 * (9.0 * square - 10.0 * frac),
        0.5 * (-9.0 * square + 8.0 * frac + 1.0),
        0.5 * (3.0 * square - 2.0 * frac),
    )


def splat(value):
    return jnp.full((8, LANES), value, F32)


def exchange(head, tail):
    count = lax.axis_size("lat")
    below = lax.ppermute(head, "lat", [(i + 1, i) for i in range(count - 1)])
    above = lax.ppermute(tail, "lat", [(i, i + 1) for i in range(count - 1)])
    return above, below


def channel_minor():
    out = lax.broadcasted_iota(jnp.int32, (LANES, LANES), 0)
    src = lax.broadcasted_iota(jnp.int32, (LANES, LANES), 1)
    return ((out % 8) * 16 + out // 8 == src).astype(F32).astype(BF16)


def lanes():
    lane = lax.broadcasted_iota(jnp.int32, (8, LANES), 1)
    return lane, lax.broadcasted_iota(jnp.int32, (8, LANES), 0)


def col_taps(values, shift):
    lane, row = lanes()
    base = jnp.zeros((8, LANES), F32)
    for tap in range(4):
        base = jnp.where(lane - row == tap, values[tap], base)
    left, right = [], []
    for group in range(0, LANES, 8):
        moved = pltpu.roll(base, (shift + group) & (LANES - 1), 1)
        inside = lane - row >= shift + group
        left.append(jnp.where(inside, moved, 0.0))
        right.append(jnp.where(inside, 0.0, moved))
    both = [jnp.concatenate(left, axis=0), jnp.concatenate(right, axis=0)]
    return jnp.concatenate(both, axis=1).astype(BF16)


REACH = BH + 4


def row_taps(values):
    lane, row = lanes()
    base = jnp.zeros((8, LANES), F32)
    for tap in range(4):
        base = jnp.where((lane - BH * row + tap) & (LANES - 1) == 0, values[tap], base)
    own = lane // BH == row
    moved = [base] + [pltpu.roll(base, step, 1) for step in range(1, REACH)]
    return jnp.concatenate([jnp.where(own, part, 0.0) for part in moved], axis=0).astype(BF16)


def pack_body(offs, srow, scol, fracs, cot, adv, head_ref, tail_ref, rows, meta, arrived, left):
    channels = cot.shape[0]
    last = offs.shape[2] - 1
    inward, outward = [], []
    for side, (out_ref, row) in enumerate(((head_ref, 0), (tail_ref, last))):
        for which, source in enumerate((cot, adv)):
            job = 2 * side + which
            inward.append(
                pltpu.make_async_copy(
                    source.at[:, row * BH : (row + 1) * BH, :], rows.at[job], arrived.at[job]
                )
            )
            place = slice(which * channels, (which + 1) * channels)
            outward.append(
                pltpu.make_async_copy(rows.at[job], out_ref.at[place], left.at[job])
            )
    for job in inward:
        job.start()
    lane = lax.broadcasted_iota(jnp.int32, (BH, LANES), 1)
    for side, (out_ref, row) in enumerate(((head_ref, 0), (tail_ref, last))):
        value = jnp.zeros((BH, LANES), F32)
        for block in range(4):
            own = [
                (BH // 2 * offs[0, block, row] + srow[block, row]).astype(F32),
                offs[1, block, row].astype(F32),
                scol[block, row].astype(F32),
                fracs[0, block, row],
                fracs[1, block, row],
            ]
            for slot, entry in enumerate(own):
                value = jnp.where(lane == block * EDGE + slot, entry, value)
        meta[side] = jnp.zeros(meta.shape[1:], BF16)
        for part in range(3):
            high = value.astype(BF16)
            meta[side, :, part * LANES : (part + 1) * LANES] = high
            value = value - high.astype(F32)
        outward.append(
            pltpu.make_async_copy(meta.at[side], out_ref.at[2 * channels], left.at[4 + side])
        )
        outward[-1].start()
    for job in range(4):
        inward[job].wait()
        outward[job].start()
    for job in outward:
        job.wait()


def pack(places, cot, adv):
    channels, _, columns = cot.shape
    shape = jax.ShapeDtypeStruct((2 * channels + 1, BH, columns), BF16)
    anywhere = pl.BlockSpec(memory_space=pl.ANY)
    return pl.pallas_call(
        pack_body,
        name="pack",
        out_shape=(shape, shape),
        grid_spec=pltpu.PrefetchScalarGridSpec(
            num_scalar_prefetch=4,
            grid=(1,),
            in_specs=[anywhere, anywhere],
            out_specs=[anywhere, anywhere],
            scratch_shapes=[
                pltpu.VMEM((4, channels, BH, columns), BF16),
                pltpu.VMEM((2, BH, columns), BF16),
                pltpu.SemaphoreType.DMA((4,)),
                pltpu.SemaphoreType.DMA((6,)),
            ],
        ),
        compiler_params=pltpu.CompilerParams(dimension_semantics=("arbitrary",)),
    )(*places, cot, adv)


def spread_blocks(jobs, tap_scr, row_scr, z_scr, acc):
    for job, (rows, block, first, py, tile, shift, wx, wy) in enumerate(jobs):
        tap_scr[job] = col_taps(wx, shift)
        row_scr[job] = row_taps(wy)
    for job, (rows, block, first, py, tile, shift, wx, wy) in enumerate(jobs):
        z = jnp.dot(halves_of(rows, block), tap_scr[job], preferred_element_type=F32)
        z_scr[job, :, 0:LANES] = z[0:LANES, 0:LANES].astype(BF16)
        middle = z[0:LANES, LANES:] + z[LANES:, 0:LANES]
        z_scr[job, :, LANES : 2 * LANES] = middle.astype(BF16)
        z_scr[job, :, 2 * LANES :] = z[LANES:, LANES:].astype(BF16)
    moved = [
        jnp.dot(row_scr[job], z_scr[job], preferred_element_type=F32) for job in range(len(jobs))
    ]
    for job, (rows, block, first, py, tile, shift, wx, wy) in enumerate(jobs):
        for part in range(3):
            target = (2 * block + 6 + part + tile) & 7
            value = moved[job][:, part * LANES : (part + 1) * LANES].reshape(REACH, 8, LANES)
            at = pl.ds(first + py, REACH)
            acc[at, target] = acc[at, target] + value


def spread_scratch():
    return [
        pltpu.VMEM((8, LANES, 2 * LANES), BF16),
        pltpu.VMEM((8, REACH * 8, LANES), BF16),
        pltpu.VMEM((8, LANES, 3 * LANES), BF16),
    ]


def halves_of(rows, block):
    return jnp.concatenate(
        [
            rows[:, block * BW : block * BW + LANES],
            rows[:, block * BW + LANES : (block + 1) * BW],
        ],
        axis=0,
    )


def emit(acc, first, out_ref):
    for tile_index in range(8):
        done = acc[pl.ds(first, BH), tile_index].reshape(BH * 8, LANES)
        out_ref[:, tile_index * LANES : (tile_index + 1) * LANES] = done.astype(BF16)


def spread_body(offs, srow, scol, fracs, cot_ref, out_ref, edge_ref, tap_scr, row_scr, z_scr, acc):
    step = pl.program_id(0)
    last = pl.num_programs(0) - 1

    @pl.when(step == 0)
    def _():
        acc[0 : 2 * BH] = jnp.zeros((2 * BH,) + acc.shape[1:], F32)

    @pl.when(step < last)
    def _():
        acc[pl.ds((2 * step + 2) * BH, 2 * BH)] = jnp.zeros((2 * BH,) + acc.shape[1:], F32)
        jobs = []
        for half in range(2):
            row = 2 * step + half
            rows = cot_ref[:, half * BH : (half + 1) * BH].reshape(LANES, cot_ref.shape[2])
            for block in range(4):
                jobs.append(
                    (
                        rows,
                        block,
                        row * BH,
                        BH // 2 * offs[0, block, row] + srow[block, row],
                        offs[1, block, row],
                        scol[block, row],
                        weights(splat(fracs[1, block, row])),
                        weights(splat(fracs[0, block, row])),
                    )
                )
        spread_blocks(jobs, tap_scr, row_scr, z_scr, acc)

    emit(acc, jnp.maximum(2 * step - 1, 0) * BH, out_ref.at[0])
    emit(acc, 2 * step * BH, out_ref.at[1])

    @pl.when(step == 0)
    def _():
        edge_ref[0] = acc[BH : 2 * BH]

    @pl.when(step == last)
    def _():
        edge_ref[0] = acc[pl.ds(2 * last * BH, BH)]


def spread(places, cot):
    channels, band_rows, columns = cot.shape
    blocks = band_rows // BH
    pairs = blocks // 2
    tiles = columns // LANES
    return pl.pallas_call(
        spread_body,
        name="spread",
        out_shape=(
            jax.ShapeDtypeStruct((blocks, BH * channels, columns), BF16),
            jax.ShapeDtypeStruct((2, BH, tiles, channels, LANES), F32),
        ),
        grid_spec=pltpu.PrefetchScalarGridSpec(
            num_scalar_prefetch=4,
            grid=(pairs + 1,),
            in_specs=[
                pl.BlockSpec(
                    (channels, 2 * BH, columns), lambda g, *a: (0, jnp.minimum(g, pairs - 1), 0)
                )
            ],
            out_specs=[
                pl.BlockSpec(
                    (2, BH * channels, columns), lambda g, *a: (jnp.maximum(g - 1, 0), 0, 0)
                ),
                pl.BlockSpec(
                    (1, BH, tiles, channels, LANES),
                    lambda g, *a: (jnp.where(g == pairs, 1, 0), 0, 0, 0, 0),
                ),
            ],
            scratch_shapes=spread_scratch()
            + [pltpu.VMEM(((blocks + 2) * BH, tiles, channels, LANES), F32)],
        ),
        compiler_params=pltpu.CompilerParams(dimension_semantics=("arbitrary",)),
    )(*places, cot)


def edge_body(meta, top_ref, bot_ref, edge_ref, whole, out_ref, tap_scr, row_scr, z_scr, acc):
    step = pl.program_id(0)
    upper, lower = 2 * BH, 3 * BH

    @pl.when(step == 0)
    def _():
        acc[0:upper] = jnp.zeros((upper,) + acc.shape[1:], F32)
        acc[upper : upper + BH] = edge_ref[0]
        acc[lower : lower + BH] = edge_ref[1]
        acc[lower + BH :] = jnp.zeros((2 * BH,) + acc.shape[1:], F32)
        jobs = []
        for side, ref in enumerate((top_ref, bot_ref)):
            rows = ref[0 : LANES // BH].reshape(LANES, ref.shape[2])
            for block in range(4):
                at = [block * EDGE + slot for slot in range(EDGE)]
                place = [meta[side, k].astype(jnp.int32) for k in at[:3]]
                fracs = [
                    meta[side, k] + meta[side, LANES + k] + meta[side, 2 * LANES + k]
                    for k in at[3:]
                ]
                wy, wx = [weights(splat(frac)) for frac in fracs]
                jobs.append((rows, block, side * lower, *place, wx, wy))
        spread_blocks(jobs, tap_scr, row_scr, z_scr, acc)

    emit(acc, upper + step * BH, out_ref.at[0])


def spread_edges(meta, top, bottom, edges, dy):
    blocks, rows, columns = dy.shape
    channels = edges.shape[3]
    return pl.pallas_call(
        edge_body,
        name="spread_edges",
        out_shape=jax.ShapeDtypeStruct(dy.shape, dy.dtype),
        grid_spec=pltpu.PrefetchScalarGridSpec(
            num_scalar_prefetch=1,
            grid=(2,),
            in_specs=[
                pl.BlockSpec((channels, BH, columns), lambda g, a: (0, 0, 0)),
                pl.BlockSpec((channels, BH, columns), lambda g, a: (0, 0, 0)),
                pl.BlockSpec(edges.shape, lambda g, a: (0, 0, 0, 0, 0)),
                pl.BlockSpec(memory_space=pl.ANY),
            ],
            out_specs=pl.BlockSpec((1, rows, columns), lambda g, a: (g * (blocks - 1), 0, 0)),
            scratch_shapes=spread_scratch() + [pltpu.VMEM((6 * BH,) + edges.shape[2:], F32)],
        ),
        input_output_aliases={4: 0},
        compiler_params=pltpu.CompilerParams(dimension_semantics=("arbitrary",)),
    )(meta, top, bottom, edges, dy)


def frac_body(
    offs, srow, scol, fracs, top_ref, mid_ref, next_ref, bot_ref, cot_ref, out_ref, cot_scr, z_scr, field
):
    step = pl.program_id(0)
    last = pl.num_programs(0) - 1
    width = cot_scr.shape[1]
    order = channel_minor()

    def put(row_block, source):
        rows = source[...].reshape(LANES, width)
        moved = jnp.dot(order, rows, preferred_element_type=F32)
        for tile_index in range(8):
            field[pl.ds(row_block * BH, BH), tile_index] = moved[
                :, tile_index * LANES : (tile_index + 1) * LANES
            ].reshape(BH, 8, LANES)

    @pl.when(step == 0)
    def _():
        put(0, top_ref)
        put(1, mid_ref)

    @pl.when(step == last)
    def _():
        put(step + 2, bot_ref)

    @pl.when(step < last)
    def _():
        put(step + 2, next_ref)

    rows = cot_ref[...].reshape(LANES, width)
    cot_scr[...] = jnp.dot(order, rows, preferred_element_type=F32).astype(BF16)
    for block in range(4):
        py = BH // 2 * offs[0, block, step] + srow[block, step]
        tile = offs[1, block, step]
        shift = scol[block, step]
        row_frac, col_frac = splat(fracs[0, block, step]), splat(fracs[1, block, step])
        both = jnp.concatenate(
            [
                col_taps(weights(col_frac), shift),
                col_taps(slopes(col_frac), shift),
            ],
            axis=1,
        )
        halves = jnp.concatenate(
            [
                cot_scr[:, block * BW : block * BW + LANES],
                cot_scr[:, block * BW + LANES : (block + 1) * BW],
            ],
            axis=0,
        )
        z_scr[block] = jnp.dot(halves, both, preferred_element_type=F32)
        by_value = [jnp.zeros((8, LANES), F32) for _ in range(4)]
        by_slope = [jnp.zeros((8, LANES), F32) for _ in range(4)]
        for part in range(3):
            pair = []
            for lane in (0, 2 * LANES):
                if part == 0:
                    z = z_scr[block, 0:LANES, lane : lane + LANES]
                elif part == 1:
                    z = (
                        z_scr[block, 0:LANES, lane + LANES : lane + 2 * LANES]
                        + z_scr[block, LANES:, lane : lane + LANES]
                    )
                else:
                    z = z_scr[block, LANES:, lane + LANES : lane + 2 * LANES]
                pair.append(z.reshape(BH, 8, LANES))
            source = (2 * block + 6 + part + tile) & 7
            for j in range(BH + 3):
                value = field[step * BH + py + j, source]
                for tap in range(4):
                    if 0 <= j - tap < BH:
                        by_value[tap] = by_value[tap] + value * pair[0][j - tap]
                        by_slope[tap] = by_slope[tap] + value * pair[1][j - tap]
        first = jnp.zeros((8, LANES), F32)
        second = jnp.zeros((8, LANES), F32)
        wy, sy = weights(row_frac), slopes(row_frac)
        for tap in range(4):
            first = first + sy[tap].astype(BF16).astype(F32) * by_value[tap]
            second = second + wy[tap].astype(BF16).astype(F32) * by_slope[tap]
        out_ref[0, block] = first
        out_ref[1, block] = second


def frac_sums(places, top, field, bottom, cot):
    channels, band_rows, columns = cot.shape
    blocks = band_rows // BH
    shape = (channels, BH, columns)
    return pl.pallas_call(
        frac_body,
        name="frac_sums",
        out_shape=jax.ShapeDtypeStruct((2, blocks * 4, 8, LANES), F32),
        grid_spec=pltpu.PrefetchScalarGridSpec(
            num_scalar_prefetch=4,
            grid=(blocks,),
            in_specs=[
                pl.BlockSpec(shape, lambda g, *a: (1, 0, 0)),
                pl.BlockSpec(shape, lambda g, *a: (0, 0, 0)),
                pl.BlockSpec(shape, lambda g, *a: (0, jnp.minimum(g + 1, blocks - 1), 0)),
                pl.BlockSpec(shape, lambda g, *a: (1, 0, 0)),
                pl.BlockSpec(shape, lambda g, *a: (0, g, 0)),
            ],
            out_specs=pl.BlockSpec((2, 4, 8, LANES), lambda g, *a: (0, g, 0, 0)),
            scratch_shapes=[
                pltpu.VMEM((BH * channels, columns), BF16),
                pltpu.VMEM((4, 2 * LANES, 4 * LANES), F32),
                pltpu.VMEM(((blocks + 2) * BH, columns // LANES, channels, LANES), F32),
            ],
        ),
        compiler_params=pltpu.CompilerParams(dimension_semantics=("arbitrary",)),
    )(*places, top, field, field, bottom, cot)


def gate_body(x_ref, w_in_t, half_bias, act_ref, slope_ref):
    part = 256
    for at in range(0, x_ref.shape[2], part):
        x = x_ref[0, :, at : at + part]
        half = jnp.dot(w_in_t[...], x, preferred_element_type=F32) + half_bias[...]
        twice = 1.0 + jnp.tanh(half)
        act = half * twice
        act_ref[0, :, at : at + part] = act.astype(BF16)
        slope_ref[0, :, at : at + part] = (twice + act * (2.0 - twice)).astype(BF16)


def gate(x, half_w_in_t, half_bias):
    rows, channels, columns = x.shape
    rows = rows // 2
    whole = lambda shape: pl.BlockSpec(shape, lambda r: (0,) * len(shape))
    tile = lambda height: pl.BlockSpec((1, height, columns), lambda r: (r, 0, 0))
    return pl.pallas_call(
        gate_body,
        name="gate",
        out_shape=(jax.ShapeDtypeStruct((rows, HID, columns), BF16),) * 2,
        grid=(rows,),
        in_specs=[
            pl.BlockSpec((1, channels, columns), lambda r: (2 * r + 1, 0, 0)),
            whole((HID, channels)),
            whole((HID, 1)),
        ],
        out_specs=[tile(HID), tile(HID)],
        compiler_params=pltpu.CompilerParams(dimension_semantics=("arbitrary",)),
    )(x, half_w_in_t, half_bias)


def mlp_body(
    x_ref, dy_ref, act_ref, slope_ref, w_in_t, half_bias, w_in, w_out, tail_ref, dx_ref, send_ref,
    g_in, g_out, g_bias, act_scr, dpre_scr
):
    step = pl.program_id(0)

    @pl.when(step == 0)
    def _():
        g_in[...] = jnp.zeros_like(g_in)
        g_out[...] = jnp.zeros_like(g_out)
        g_bias[...] = jnp.zeros_like(g_bias)

    part = 256
    points = (((1,), (1,)), ((), ()))

    def field(item):
        row, cut = item
        return dy_ref[:, row, :, cut].reshape(C, part)

    def gates(item, slot):
        row, cut = item
        if row == 0:
            half = jnp.dot(w_in_t[...], x_ref[0, :, cut], preferred_element_type=F32)
            half = half + half_bias[...]
            twice = 1.0 + jnp.tanh(half)
            act = half * twice
            act_scr[slot] = act.astype(BF16)
            slope = twice + act * (2.0 - twice)
        else:
            slope = slope_ref[0, :, cut].astype(F32)
        dact = jnp.dot(w_out[...], field(item), preferred_element_type=F32)
        dpre = (dact * slope).astype(BF16)
        dpre_scr[slot] = dpre
        total = g_bias[...]
        for lane in range(0, part, LANES):
            total = total + dpre[:, lane : lane + LANES].astype(F32)
        g_bias[...] = total

    def products(item, slot):
        row, cut = item
        dy = field(item)
        dpre = dpre_scr[slot]
        dx = dy.astype(F32) + jnp.dot(w_in[...], dpre, preferred_element_type=F32)
        dx_ref[row, :, cut] = dx.astype(BF16)
        g_in[...] += lax.dot_general(dpre, x_ref[row, :, cut], points, preferred_element_type=F32)
        act = act_scr[slot] if row == 0 else act_ref[0, :, cut]
        g_out[...] += lax.dot_general(act, dy, points, preferred_element_type=F32)

    items = []
    for at in range(0, x_ref.shape[2], part):
        items.extend([(0, slice(at, at + part)), (1, slice(at, at + part))])
    gates(items[0], 0)
    for index in range(1, len(items)):
        gates(items[index], index % 3)
        products(items[index - 1], (index - 1) % 3)
    products(items[-1], (len(items) - 1) % 3)

    @pl.when(step == pl.num_programs(0) - 1)
    def _():
        parts, each, lanes = send_ref.shape
        shift = jnp.sum(g_bias[...], axis=1, keepdims=True)
        high = shift.astype(BF16).astype(F32)
        lane = lax.broadcasted_iota(jnp.int32, (HID, LANES), 1)
        tail = jnp.where(lane == 0, high, jnp.where(lane == 1, shift - high, tail_ref[...]))
        send = jnp.concatenate([g_in[...], g_out[...], tail], axis=1)
        send_ref[...] = send.reshape(parts, each, lanes).astype(BF16)


def mlp(x, dy, act, slope, half_w_in_t, half_bias, w_in, w_out, tail, parts):
    rows, channels, columns = x.shape
    sources = dy.shape[0]
    whole = lambda shape: pl.BlockSpec(shape, lambda r: (0,) * len(shape))
    pair = pl.BlockSpec((2, channels, columns), lambda r: (r, 0, 0))
    ready = pl.BlockSpec((1, HID, columns), lambda r: (r, 0, 0))
    send = (parts, HID // parts, 2 * channels + LANES)
    return pl.pallas_call(
        mlp_body,
        name="mlp",
        out_shape=(
            jax.ShapeDtypeStruct((rows, channels, columns), BF16),
            jax.ShapeDtypeStruct(send, BF16),
        ),
        grid=(rows // 2,),
        in_specs=[
            pair,
            pl.BlockSpec((sources, 2, 8, columns), lambda r: (0, r, 0, 0)),
            ready,
            ready,
            whole((HID, channels)),
            whole((HID, 1)),
            whole((channels, HID)),
            whole((HID, channels)),
            whole((HID, LANES)),
        ],
        out_specs=[pair, whole(send)],
        scratch_shapes=[
            pltpu.VMEM((HID, channels), F32),
            pltpu.VMEM((HID, channels), F32),
            pltpu.VMEM((HID, LANES), F32),
            pltpu.VMEM((3, HID, 256), BF16),
            pltpu.VMEM((3, HID, 256), BF16),
        ],
        compiler_params=pltpu.CompilerParams(dimension_semantics=("arbitrary",)),
    )(x, dy, act, slope, half_w_in_t, half_bias, w_in, w_out * jnp.asarray(0.5, BF16), tail)


def finish_body(scale, frac_scale, got_ref, first_ref, second_ref, shift_ref, frac_ref):
    total = got_ref[...]
    each = total.shape[0]
    held = 2 * frac_ref.shape[2]
    first_ref[...] = total[:, 0:C] * scale
    second_ref[...] = total[:, C : 2 * C] * scale
    tail = total[:, 2 * C :]
    lane = lax.broadcasted_iota(jnp.int32, (each, LANES), 1)
    row = lax.broadcasted_iota(jnp.int32, (each, LANES), 0)
    shift = tail[:, 0:1] + tail[:, 1:2]
    shift = jnp.sum(jnp.where(lane == row, shift, 0.0), axis=0, keepdims=True)
    shift_ref[...] = shift[:, 0:each] * scale
    frac = tail[:, held : 2 * held] + tail[:, 2 * held : 3 * held]
    half = held // 2
    frac_ref[0] = frac[:, 0:half] * frac_scale
    frac_ref[1] = frac[:, half:] * frac_scale


def finish(got, scale, frac_scale, row_blocks):
    each = got.shape[0]
    return pl.pallas_call(
        functools.partial(finish_body, scale, frac_scale),
        name="finish",
        out_shape=(
            jax.ShapeDtypeStruct((each, C), F32),
            jax.ShapeDtypeStruct((each, C), F32),
            jax.ShapeDtypeStruct((1, each), F32),
            jax.ShapeDtypeStruct((2, each, row_blocks), F32),
        ),
        in_specs=[pl.BlockSpec(memory_space=pltpu.VMEM)],
    )(got)


def shards(
    inputs, w_in, bias_in, w_out, advected, cotangent, offsets, stencil_row, stencil_col, fracs
):
    channels_dev, band_rows, columns = advected.shape
    row_blocks = band_rows // BH
    point_rows = inputs.shape[1]
    lat = lax.axis_size("lat")
    grp = lax.axis_size("grp")

    places = (
        offsets.transpose(0, 2, 1),
        stencil_row.T,
        stencil_col.T,
        fracs.transpose(0, 2, 1),
    )
    head, tail = pack(places, cotangent, advected)
    top, bottom = exchange(head, tail)
    dy_band, edges = spread(places, cotangent)
    meta = jnp.stack([halo[2 * channels_dev, 0, : 3 * LANES] for halo in (top, bottom)])
    dy_band = spread_edges(meta.astype(F32), top, bottom, edges, dy_band)
    dy_send = dy_band.reshape(grp, point_rows, channels_dev, columns)
    dy_points = lax.all_to_all(dy_send, "grp", split_axis=0, concat_axis=0, tiled=True)

    frac_parts = frac_sums(places, top, advected, bottom, cotangent)
    parts = lat * grp
    each = HID // parts
    held = 2 * row_blocks
    frac_local = jnp.sum(frac_parts, axis=(2, 3)).reshape(held, columns // BW).T
    high = lax.reduce_precision(frac_local, 8, 7)
    both = jnp.stack([high, frac_local - high], axis=1)
    mine = jnp.where(jnp.arange(lat) == lax.axis_index("lat"), 1.0, 0.0)
    slots = mine[:, None, None, None] * both.reshape(1, 1, each, 2 * held)
    slots = jnp.broadcast_to(slots, (lat, grp, each, 2 * held)).reshape(HID, 2 * held)
    extra = jnp.pad(slots, ((0, 0), (held, LANES - 3 * held)))

    x_rows = inputs.transpose(1, 0, 2)
    half_w_in_t = w_in.T * jnp.asarray(0.5, BF16)
    half_bias = 0.5 * bias_in[:, None]
    act, slope = gate(x_rows, half_w_in_t, half_bias)
    dx_rows, send = mlp(
        x_rows, dy_points, act, slope, half_w_in_t, half_bias, w_in, w_out, extra, parts
    )
    grad_inputs = dx_rows.transpose(1, 0, 2)

    got = lax.all_to_all(send, ("lat", "grp"), split_axis=0, concat_axis=0, tiled=True)
    scale = 1.0 / math.sqrt(point_rows * columns * parts)
    first, second, shift, frac = finish(jnp.sum(got.astype(F32), axis=0), scale, 1.0 / math.sqrt(C * BH * BW), row_blocks)
    return (grad_inputs, first.T, shift.reshape(each), second, frac.transpose(0, 2, 1))


def solution(mesh):
    placed = (
        P(None, ("lat", "grp"), None),
        P(),
        P(),
        P(),
        P("grp", "lat", None),
        P("grp", "lat", None),
        P(None, "lat", None),
        P("lat", None),
        P("lat", None),
        P(None, "lat", None),
    )
    return jax.shard_map(
        shards,
        mesh=mesh,
        in_specs=placed,
        out_specs=(
            P(None, ("lat", "grp"), None),
            P(None, ("lat", "grp")),
            P(("lat", "grp")),
            P(("lat", "grp"), None),
            P(None, "lat", None),
        ),
        check_vma=False,
    )
```

```python
import functools
import math

import jax
import jax.numpy as jnp
from jax import lax
from jax.experimental import pallas as pl
from jax.experimental.pallas import tpu as pltpu
from jax.sharding import PartitionSpec as P


C = 256
BH = 16
BW = 256
LANES = 128
HID = 512
F32 = jnp.float32
BF16 = jnp.bfloat16


EDGE = 5


def weights(frac):
    square = frac * frac
    cube = square * frac
    return (
        0.5 * (-cube + 2.0 * square - frac),
        0.5 * (3.0 * cube - 5.0 * square + 2.0),
        0.5 * (-3.0 * cube + 4.0 * square + frac),
        0.5 * (cube - square),
    )


def slopes(frac):
    square = frac * frac
    return (
        0.5 * (-3.0 * square + 4.0 * frac - 1.0),
        0.5 * (9.0 * square - 10.0 * frac),
        0.5 * (-9.0 * square + 8.0 * frac + 1.0),
        0.5 * (3.0 * square - 2.0 * frac),
    )


def splat(value):
    return jnp.full((8, LANES), value, F32)


def exchange(head, tail):
    count = lax.axis_size("lat")
    below = lax.ppermute(head, "lat", [(i + 1, i) for i in range(count - 1)])
    above = lax.ppermute(tail, "lat", [(i, i + 1) for i in range(count - 1)])
    return above, below


def channel_minor():
    out = lax.broadcasted_iota(jnp.int32, (LANES, LANES), 0)
    src = lax.broadcasted_iota(jnp.int32, (LANES, LANES), 1)
    return ((out % 8) * 16 + out // 8 == src).astype(F32).astype(BF16)


def lanes():
    lane = lax.broadcasted_iota(jnp.int32, (8, LANES), 1)
    return lane, lax.broadcasted_iota(jnp.int32, (8, LANES), 0)


def col_taps(values, shift):
    lane, row = lanes()
    base = jnp.zeros((8, LANES), F32)
    for tap in range(4):
        base = jnp.where(lane - row == tap, values[tap], base)
    left, right = [], []
    for group in range(0, LANES, 8):
        moved = pltpu.roll(base, (shift + group) & (LANES - 1), 1)
        inside = lane - row >= shift + group
        left.append(jnp.where(inside, moved, 0.0))
        right.append(jnp.where(inside, 0.0, moved))
    both = [jnp.concatenate(left, axis=0), jnp.concatenate(right, axis=0)]
    return jnp.concatenate(both, axis=1).astype(BF16)


REACH = BH + 4


def row_taps(values):
    lane, row = lanes()
    base = jnp.zeros((8, LANES), F32)
    for tap in range(4):
        base = jnp.where((lane - BH * row + tap) & (LANES - 1) == 0, values[tap], base)
    own = lane // BH == row
    moved = [base] + [pltpu.roll(base, step, 1) for step in range(1, REACH)]
    return jnp.concatenate([jnp.where(own, part, 0.0) for part in moved], axis=0).astype(BF16)


def pack_body(offs, srow, scol, fracs, cot, adv, head_ref, tail_ref, rows, meta, arrived, left):
    channels = cot.shape[0]
    last = offs.shape[2] - 1
    inward, outward = [], []
    for side, (out_ref, row) in enumerate(((head_ref, 0), (tail_ref, last))):
        for which, source in enumerate((cot, adv)):
            job = 2 * side + which
            inward.append(
                pltpu.make_async_copy(
                    source.at[:, row * BH : (row + 1) * BH, :], rows.at[job], arrived.at[job]
                )
            )
            place = slice(which * channels, (which + 1) * channels)
            outward.append(
                pltpu.make_async_copy(rows.at[job], out_ref.at[place], left.at[job])
            )
    for job in inward:
        job.start()
    lane = lax.broadcasted_iota(jnp.int32, (BH, LANES), 1)
    for side, (out_ref, row) in enumerate(((head_ref, 0), (tail_ref, last))):
        value = jnp.zeros((BH, LANES), F32)
        for block in range(4):
            own = [
                (BH // 2 * offs[0, block, row] + srow[block, row]).astype(F32),
                offs[1, block, row].astype(F32),
                scol[block, row].astype(F32),
                fracs[0, block, row],
                fracs[1, block, row],
            ]
            for slot, entry in enumerate(own):
                value = jnp.where(lane == block * EDGE + slot, entry, value)
        meta[side] = jnp.zeros(meta.shape[1:], BF16)
        for part in range(3):
            high = value.astype(BF16)
            meta[side, :, part * LANES : (part + 1) * LANES] = high
            value = value - high.astype(F32)
        outward.append(
            pltpu.make_async_copy(meta.at[side], out_ref.at[2 * channels], left.at[4 + side])
        )
        outward[-1].start()
    for job in range(4):
        inward[job].wait()
        outward[job].start()
    for job in outward:
        job.wait()


def pack(places, cot, adv):
    channels, _, columns = cot.shape
    shape = jax.ShapeDtypeStruct((2 * channels + 1, BH, columns), BF16)
    anywhere = pl.BlockSpec(memory_space=pl.ANY)
    return pl.pallas_call(
        pack_body,
        name="pack",
        out_shape=(shape, shape),
        grid_spec=pltpu.PrefetchScalarGridSpec(
            num_scalar_prefetch=4,
            grid=(1,),
            in_specs=[anywhere, anywhere],
            out_specs=[anywhere, anywhere],
            scratch_shapes=[
                pltpu.VMEM((4, channels, BH, columns), BF16),
                pltpu.VMEM((2, BH, columns), BF16),
                pltpu.SemaphoreType.DMA((4,)),
                pltpu.SemaphoreType.DMA((6,)),
            ],
        ),
        compiler_params=pltpu.CompilerParams(dimension_semantics=("arbitrary",)),
    )(*places, cot, adv)


def spread_blocks(jobs, tap_scr, row_scr, z_scr, acc):
    for job, (rows, block, first, py, tile, shift, wx, wy) in enumerate(jobs):
        tap_scr[job] = col_taps(wx, shift)
        row_scr[job] = row_taps(wy)
    for job, (rows, block, first, py, tile, shift, wx, wy) in enumerate(jobs):
        z = jnp.dot(halves_of(rows, block), tap_scr[job], preferred_element_type=F32)
        z_scr[job, :, 0:LANES] = z[0:LANES, 0:LANES].astype(BF16)
        middle = z[0:LANES, LANES:] + z[LANES:, 0:LANES]
        z_scr[job, :, LANES : 2 * LANES] = middle.astype(BF16)
        z_scr[job, :, 2 * LANES :] = z[LANES:, LANES:].astype(BF16)
    moved = [
        jnp.dot(row_scr[job], z_scr[job], preferred_element_type=F32) for job in range(len(jobs))
    ]
    for job, (rows, block, first, py, tile, shift, wx, wy) in enumerate(jobs):
        for part in range(3):
            target = (2 * block + 6 + part + tile) & 7
            value = moved[job][:, part * LANES : (part + 1) * LANES].reshape(REACH, 8, LANES)
            at = pl.ds(first + py, REACH)
            acc[at, target] = acc[at, target] + value


def spread_scratch():
    return [
        pltpu.VMEM((16, LANES, 2 * LANES), BF16),
        pltpu.VMEM((16, REACH * 8, LANES), BF16),
        pltpu.VMEM((16, LANES, 3 * LANES), BF16),
    ]


def halves_of(rows, block):
    return jnp.concatenate(
        [
            rows[:, block * BW : block * BW + LANES],
            rows[:, block * BW + LANES : (block + 1) * BW],
        ],
        axis=0,
    )


def emit(acc, first, out_ref):
    for tile_index in range(8):
        done = acc[pl.ds(first, BH), tile_index].reshape(BH * 8, LANES)
        out_ref[:, tile_index * LANES : (tile_index + 1) * LANES] = done.astype(BF16)


def spread_body(offs, srow, scol, fracs, cot_ref, out_ref, edge_ref, tap_scr, row_scr, z_scr, acc):
    step = pl.program_id(0)
    last = pl.num_programs(0) - 1

    @pl.when(step == 0)
    def _():
        acc[0 : 2 * BH] = jnp.zeros((2 * BH,) + acc.shape[1:], F32)

    @pl.when(step < last)
    def _():
        acc[pl.ds((4 * step + 2) * BH, 4 * BH)] = jnp.zeros((4 * BH,) + acc.shape[1:], F32)
        jobs = []
        for half in range(4):
            row = 4 * step + half
            rows = cot_ref[:, half * BH : (half + 1) * BH].reshape(LANES, cot_ref.shape[2])
            for block in range(4):
                jobs.append(
                    (
                        rows,
                        block,
                        row * BH,
                        BH // 2 * offs[0, block, row] + srow[block, row],
                        offs[1, block, row],
                        scol[block, row],
                        weights(splat(fracs[1, block, row])),
                        weights(splat(fracs[0, block, row])),
                    )
                )
        spread_blocks(jobs, tap_scr, row_scr, z_scr, acc)

    for slot in range(4):
        emit(acc, jnp.maximum(4 * step - 3 + slot, 0) * BH, out_ref.at[slot])

    @pl.when(step == 0)
    def _():
        edge_ref[0] = acc[BH : 2 * BH]

    @pl.when(step == last)
    def _():
        edge_ref[0] = acc[pl.ds(4 * last * BH, BH)]


def spread(places, cot):
    channels, band_rows, columns = cot.shape
    blocks = band_rows // BH
    quads = blocks // 4
    tiles = columns // LANES
    return pl.pallas_call(
        spread_body,
        name="spread",
        out_shape=(
            jax.ShapeDtypeStruct((blocks, BH * channels, columns), BF16),
            jax.ShapeDtypeStruct((2, BH, tiles, channels, LANES), F32),
        ),
        grid_spec=pltpu.PrefetchScalarGridSpec(
            num_scalar_prefetch=4,
            grid=(quads + 1,),
            in_specs=[
                pl.BlockSpec(
                    (channels, 4 * BH, columns), lambda g, *a: (0, jnp.minimum(g, quads - 1), 0)
                )
            ],
            out_specs=[
                pl.BlockSpec(
                    (4, BH * channels, columns), lambda g, *a: (jnp.maximum(g - 1, 0), 0, 0)
                ),
                pl.BlockSpec(
                    (1, BH, tiles, channels, LANES),
                    lambda g, *a: (jnp.where(g == quads, 1, 0), 0, 0, 0, 0),
                ),
            ],
            scratch_shapes=spread_scratch()
            + [pltpu.VMEM(((blocks + 2) * BH, tiles, channels, LANES), F32)],
        ),
        compiler_params=pltpu.CompilerParams(dimension_semantics=("arbitrary",)),
    )(*places, cot)


def edge_body(meta, top_ref, bot_ref, edge_ref, whole, out_ref, tap_scr, row_scr, z_scr, acc):
    step = pl.program_id(0)
    upper, lower = 2 * BH, 3 * BH

    @pl.when(step == 0)
    def _():
        acc[0:upper] = jnp.zeros((upper,) + acc.shape[1:], F32)
        acc[upper : upper + BH] = edge_ref[0]
        acc[lower : lower + BH] = edge_ref[1]
        acc[lower + BH :] = jnp.zeros((2 * BH,) + acc.shape[1:], F32)
        jobs = []
        for side, ref in enumerate((top_ref, bot_ref)):
            rows = ref[0 : LANES // BH].reshape(LANES, ref.shape[2])
            for block in range(4):
                at = [block * EDGE + slot for slot in range(EDGE)]
                place = [meta[side, k].astype(jnp.int32) for k in at[:3]]
                fracs = [
                    meta[side, k] + meta[side, LANES + k] + meta[side, 2 * LANES + k]
                    for k in at[3:]
                ]
                wy, wx = [weights(splat(frac)) for frac in fracs]
                jobs.append((rows, block, side * lower, *place, wx, wy))
        spread_blocks(jobs, tap_scr, row_scr, z_scr, acc)

    emit(acc, upper + step * BH, out_ref.at[0])


def spread_edges(meta, top, bottom, edges, dy):
    blocks, rows, columns = dy.shape
    channels = edges.shape[3]
    return pl.pallas_call(
        edge_body,
        name="spread_edges",
        out_shape=jax.ShapeDtypeStruct(dy.shape, dy.dtype),
        grid_spec=pltpu.PrefetchScalarGridSpec(
            num_scalar_prefetch=1,
            grid=(2,),
            in_specs=[
                pl.BlockSpec((channels, BH, columns), lambda g, a: (0, 0, 0)),
                pl.BlockSpec((channels, BH, columns), lambda g, a: (0, 0, 0)),
                pl.BlockSpec(edges.shape, lambda g, a: (0, 0, 0, 0, 0)),
                pl.BlockSpec(memory_space=pl.ANY),
            ],
            out_specs=pl.BlockSpec((1, rows, columns), lambda g, a: (g * (blocks - 1), 0, 0)),
            scratch_shapes=spread_scratch() + [pltpu.VMEM((6 * BH,) + edges.shape[2:], F32)],
        ),
        input_output_aliases={4: 0},
        compiler_params=pltpu.CompilerParams(dimension_semantics=("arbitrary",)),
    )(meta, top, bottom, edges, dy)


def frac_body(
    offs, srow, scol, fracs, top_ref, mid_ref, next_ref, bot_ref, cot_ref, out_ref, cot_scr, z_scr, field
):
    step = pl.program_id(0)
    last = pl.num_programs(0) - 1
    width = cot_scr.shape[1]
    order = channel_minor()

    def put(row_block, source):
        rows = source[...].reshape(LANES, width)
        moved = jnp.dot(order, rows, preferred_element_type=F32)
        for tile_index in range(8):
            field[pl.ds(row_block * BH, BH), tile_index] = moved[
                :, tile_index * LANES : (tile_index + 1) * LANES
            ].reshape(BH, 8, LANES)

    @pl.when(step == 0)
    def _():
        put(0, top_ref)
        put(1, mid_ref)

    @pl.when(step == last)
    def _():
        put(step + 2, bot_ref)

    @pl.when(step < last)
    def _():
        put(step + 2, next_ref)

    rows = cot_ref[...].reshape(LANES, width)
    cot_scr[...] = jnp.dot(order, rows, preferred_element_type=F32).astype(BF16)
    for block in range(4):
        py = BH // 2 * offs[0, block, step] + srow[block, step]
        tile = offs[1, block, step]
        shift = scol[block, step]
        row_frac, col_frac = splat(fracs[0, block, step]), splat(fracs[1, block, step])
        both = jnp.concatenate(
            [
                col_taps(weights(col_frac), shift),
                col_taps(slopes(col_frac), shift),
            ],
            axis=1,
        )
        halves = jnp.concatenate(
            [
                cot_scr[:, block * BW : block * BW + LANES],
                cot_scr[:, block * BW + LANES : (block + 1) * BW],
            ],
            axis=0,
        )
        z_scr[block] = jnp.dot(halves, both, preferred_element_type=F32)
        by_value = [jnp.zeros((8, LANES), F32) for _ in range(4)]
        by_slope = [jnp.zeros((8, LANES), F32) for _ in range(4)]
        for part in range(3):
            pair = []
            for lane in (0, 2 * LANES):
                if part == 0:
                    z = z_scr[block, 0:LANES, lane : lane + LANES]
                elif part == 1:
                    z = (
                        z_scr[block, 0:LANES, lane + LANES : lane + 2 * LANES]
                        + z_scr[block, LANES:, lane : lane + LANES]
                    )
                else:
                    z = z_scr[block, LANES:, lane + LANES : lane + 2 * LANES]
                pair.append(z.reshape(BH, 8, LANES))
            source = (2 * block + 6 + part + tile) & 7
            for j in range(BH + 3):
                value = field[step * BH + py + j, source]
                for tap in range(4):
                    if 0 <= j - tap < BH:
                        by_value[tap] = by_value[tap] + value * pair[0][j - tap]
                        by_slope[tap] = by_slope[tap] + value * pair[1][j - tap]
        first = jnp.zeros((8, LANES), F32)
        second = jnp.zeros((8, LANES), F32)
        wy, sy = weights(row_frac), slopes(row_frac)
        for tap in range(4):
            first = first + sy[tap].astype(BF16).astype(F32) * by_value[tap]
            second = second + wy[tap].astype(BF16).astype(F32) * by_slope[tap]
        out_ref[0, block] = first
        out_ref[1, block] = second


def frac_sums(places, top, field, bottom, cot):
    channels, band_rows, columns = cot.shape
    blocks = band_rows // BH
    shape = (channels, BH, columns)
    return pl.pallas_call(
        frac_body,
        name="frac_sums",
        out_shape=jax.ShapeDtypeStruct((2, blocks * 4, 8, LANES), F32),
        grid_spec=pltpu.PrefetchScalarGridSpec(
            num_scalar_prefetch=4,
            grid=(blocks,),
            in_specs=[
                pl.BlockSpec(shape, lambda g, *a: (1, 0, 0)),
                pl.BlockSpec(shape, lambda g, *a: (0, 0, 0)),
                pl.BlockSpec(shape, lambda g, *a: (0, jnp.minimum(g + 1, blocks - 1), 0)),
                pl.BlockSpec(shape, lambda g, *a: (1, 0, 0)),
                pl.BlockSpec(shape, lambda g, *a: (0, g, 0)),
            ],
            out_specs=pl.BlockSpec((2, 4, 8, LANES), lambda g, *a: (0, g, 0, 0)),
            scratch_shapes=[
                pltpu.VMEM((BH * channels, columns), BF16),
                pltpu.VMEM((4, 2 * LANES, 4 * LANES), F32),
                pltpu.VMEM(((blocks + 2) * BH, columns // LANES, channels, LANES), F32),
            ],
        ),
        compiler_params=pltpu.CompilerParams(dimension_semantics=("arbitrary",)),
    )(*places, top, field, field, bottom, cot)


def gate_body(x_ref, w_in_t, half_bias, act_ref, slope_ref):
    part = 256
    for at in range(0, x_ref.shape[2], part):
        x = x_ref[0, :, at : at + part]
        half = jnp.dot(w_in_t[...], x, preferred_element_type=F32) + half_bias[...]
        twice = 1.0 + jnp.tanh(half)
        act = half * twice
        act_ref[0, :, at : at + part] = act.astype(BF16)
        slope_ref[0, :, at : at + part] = (twice + act * (2.0 - twice)).astype(BF16)


def gate(x, half_w_in_t, half_bias):
    rows, channels, columns = x.shape
    rows = rows // 2
    whole = lambda shape: pl.BlockSpec(shape, lambda r: (0,) * len(shape))
    tile = lambda height: pl.BlockSpec((1, height, columns), lambda r: (r, 0, 0))
    return pl.pallas_call(
        gate_body,
        name="gate",
        out_shape=(jax.ShapeDtypeStruct((rows, HID, columns), BF16),) * 2,
        grid=(rows,),
        in_specs=[
            pl.BlockSpec((1, channels, columns), lambda r: (2 * r + 1, 0, 0)),
            whole((HID, channels)),
            whole((HID, 1)),
        ],
        out_specs=[tile(HID), tile(HID)],
        compiler_params=pltpu.CompilerParams(dimension_semantics=("arbitrary",)),
    )(x, half_w_in_t, half_bias)


def mlp_body(
    x_ref, dy_ref, act_ref, slope_ref, w_in_t, half_bias, w_in, w_out, tail_ref, dx_ref, send_ref,
    g_in, g_out, g_bias, act_scr, dpre_scr
):
    step = pl.program_id(0)

    @pl.when(step == 0)
    def _():
        g_in[...] = jnp.zeros_like(g_in)
        g_out[...] = jnp.zeros_like(g_out)
        g_bias[...] = jnp.zeros_like(g_bias)

    part = 256
    points = (((1,), (1,)), ((), ()))

    def field(item):
        row, cut = item
        return dy_ref[:, row, :, cut].reshape(C, part)

    def gates(item, slot):
        row, cut = item
        if row == 0:
            half = jnp.dot(w_in_t[...], x_ref[0, :, cut], preferred_element_type=F32)
            half = half + half_bias[...]
            twice = 1.0 + jnp.tanh(half)
            act = half * twice
            act_scr[slot] = act.astype(BF16)
            slope = twice + act * (2.0 - twice)
        else:
            slope = slope_ref[0, :, cut].astype(F32)
        dact = jnp.dot(w_out[...], field(item), preferred_element_type=F32)
        dpre = (dact * slope).astype(BF16)
        dpre_scr[slot] = dpre
        total = g_bias[...]
        for lane in range(0, part, LANES):
            total = total + dpre[:, lane : lane + LANES].astype(F32)
        g_bias[...] = total

    def products(item, slot):
        row, cut = item
        dy = field(item)
        dpre = dpre_scr[slot]
        dx = dy.astype(F32) + jnp.dot(w_in[...], dpre, preferred_element_type=F32)
        dx_ref[row, :, cut] = dx.astype(BF16)
        g_in[...] += lax.dot_general(dpre, x_ref[row, :, cut], points, preferred_element_type=F32)
        act = act_scr[slot] if row == 0 else act_ref[0, :, cut]
        g_out[...] += lax.dot_general(act, dy, points, preferred_element_type=F32)

    items = []
    for at in range(0, x_ref.shape[2], part):
        items.extend([(0, slice(at, at + part)), (1, slice(at, at + part))])
    gates(items[0], 0)
    for index in range(1, len(items)):
        gates(items[index], index % 3)
        products(items[index - 1], (index - 1) % 3)
    products(items[-1], (len(items) - 1) % 3)

    @pl.when(step == pl.num_programs(0) - 1)
    def _():
        parts, each, lanes = send_ref.shape
        shift = jnp.sum(g_bias[...], axis=1, keepdims=True)
        high = shift.astype(BF16).astype(F32)
        lane = lax.broadcasted_iota(jnp.int32, (HID, LANES), 1)
        tail = jnp.where(lane == 0, high, jnp.where(lane == 1, shift - high, tail_ref[...]))
        send = jnp.concatenate([g_in[...], g_out[...], tail], axis=1)
        send_ref[...] = send.reshape(parts, each, lanes).astype(BF16)


def mlp(x, dy, act, slope, half_w_in_t, half_bias, w_in, w_out, tail, parts):
    rows, channels, columns = x.shape
    sources = dy.shape[0]
    whole = lambda shape: pl.BlockSpec(shape, lambda r: (0,) * len(shape))
    pair = pl.BlockSpec((2, channels, columns), lambda r: (r, 0, 0))
    ready = pl.BlockSpec((1, HID, columns), lambda r: (r, 0, 0))
    send = (parts, HID // parts, 2 * channels + LANES)
    return pl.pallas_call(
        mlp_body,
        name="mlp",
        out_shape=(
            jax.ShapeDtypeStruct((rows, channels, columns), BF16),
            jax.ShapeDtypeStruct(send, BF16),
        ),
        grid=(rows // 2,),
        in_specs=[
            pair,
            pl.BlockSpec((sources, 2, 8, columns), lambda r: (0, r, 0, 0)),
            ready,
            ready,
            whole((HID, channels)),
            whole((HID, 1)),
            whole((channels, HID)),
            whole((HID, channels)),
            whole((HID, LANES)),
        ],
        out_specs=[pair, whole(send)],
        scratch_shapes=[
            pltpu.VMEM((HID, channels), F32),
            pltpu.VMEM((HID, channels), F32),
            pltpu.VMEM((HID, LANES), F32),
            pltpu.VMEM((3, HID, 256), BF16),
            pltpu.VMEM((3, HID, 256), BF16),
        ],
        compiler_params=pltpu.CompilerParams(dimension_semantics=("arbitrary",)),
    )(x, dy, act, slope, half_w_in_t, half_bias, w_in, w_out * jnp.asarray(0.5, BF16), tail)


def finish_body(scale, frac_scale, got_ref, first_ref, second_ref, shift_ref, frac_ref):
    total = got_ref[...]
    each = total.shape[0]
    held = 2 * frac_ref.shape[2]
    first_ref[...] = total[:, 0:C] * scale
    second_ref[...] = total[:, C : 2 * C] * scale
    tail = total[:, 2 * C :]
    lane = lax.broadcasted_iota(jnp.int32, (each, LANES), 1)
    row = lax.broadcasted_iota(jnp.int32, (each, LANES), 0)
    shift = tail[:, 0:1] + tail[:, 1:2]
    shift = jnp.sum(jnp.where(lane == row, shift, 0.0), axis=0, keepdims=True)
    shift_ref[...] = shift[:, 0:each] * scale
    frac = tail[:, held : 2 * held] + tail[:, 2 * held : 3 * held]
    half = held // 2
    frac_ref[0] = frac[:, 0:half] * frac_scale
    frac_ref[1] = frac[:, half:] * frac_scale


def finish(got, scale, frac_scale, row_blocks):
    each = got.shape[0]
    return pl.pallas_call(
        functools.partial(finish_body, scale, frac_scale),
        name="finish",
        out_shape=(
            jax.ShapeDtypeStruct((each, C), F32),
            jax.ShapeDtypeStruct((each, C), F32),
            jax.ShapeDtypeStruct((1, each), F32),
            jax.ShapeDtypeStruct((2, each, row_blocks), F32),
        ),
        in_specs=[pl.BlockSpec(memory_space=pltpu.VMEM)],
    )(got)


def shards(
    inputs, w_in, bias_in, w_out, advected, cotangent, offsets, stencil_row, stencil_col, fracs
):
    channels_dev, band_rows, columns = advected.shape
    row_blocks = band_rows // BH
    point_rows = inputs.shape[1]
    lat = lax.axis_size("lat")
    grp = lax.axis_size("grp")

    places = (
        offsets.transpose(0, 2, 1),
        stencil_row.T,
        stencil_col.T,
        fracs.transpose(0, 2, 1),
    )
    head, tail = pack(places, cotangent, advected)
    top, bottom = exchange(head, tail)
    dy_band, edges = spread(places, cotangent)
    meta = jnp.stack([halo[2 * channels_dev, 0, : 3 * LANES] for halo in (top, bottom)])
    dy_band = spread_edges(meta.astype(F32), top, bottom, edges, dy_band)
    dy_send = dy_band.reshape(grp, point_rows, channels_dev, columns)
    dy_points = lax.all_to_all(dy_send, "grp", split_axis=0, concat_axis=0, tiled=True)

    frac_parts = frac_sums(places, top, advected, bottom, cotangent)
    parts = lat * grp
    each = HID // parts
    held = 2 * row_blocks
    frac_local = jnp.sum(frac_parts, axis=(2, 3)).reshape(held, columns // BW).T
    high = lax.reduce_precision(frac_local, 8, 7)
    both = jnp.stack([high, frac_local - high], axis=1)
    mine = jnp.where(jnp.arange(lat) == lax.axis_index("lat"), 1.0, 0.0)
    slots = mine[:, None, None, None] * both.reshape(1, 1, each, 2 * held)
    slots = jnp.broadcast_to(slots, (lat, grp, each, 2 * held)).reshape(HID, 2 * held)
    extra = jnp.pad(slots, ((0, 0), (held, LANES - 3 * held)))

    x_rows = inputs.transpose(1, 0, 2)
    half_w_in_t = w_in.T * jnp.asarray(0.5, BF16)
    half_bias = 0.5 * bias_in[:, None]
    act, slope = gate(x_rows, half_w_in_t, half_bias)
    dx_rows, send = mlp(
        x_rows, dy_points, act, slope, half_w_in_t, half_bias, w_in, w_out, extra, parts
    )
    grad_inputs = dx_rows.transpose(1, 0, 2)

    got = lax.all_to_all(send, ("lat", "grp"), split_axis=0, concat_axis=0, tiled=True)
    scale = 1.0 / math.sqrt(point_rows * columns * parts)
    first, second, shift, frac = finish(jnp.sum(got.astype(F32), axis=0), scale, 1.0 / math.sqrt(C * BH * BW), row_blocks)
    return (grad_inputs, first.T, shift.reshape(each), second, frac.transpose(0, 2, 1))


def solution(mesh):
    placed = (
        P(None, ("lat", "grp"), None),
        P(),
        P(),
        P(),
        P("grp", "lat", None),
        P("grp", "lat", None),
        P(None, "lat", None),
        P("lat", None),
        P("lat", None),
        P(None, "lat", None),
    )
    return jax.shard_map(
        shards,
        mesh=mesh,
        in_specs=placed,
        out_specs=(
            P(None, ("lat", "grp"), None),
            P(None, ("lat", "grp")),
            P(("lat", "grp")),
            P(("lat", "grp"), None),
            P(None, "lat", None),
        ),
        check_vma=False,
    )
```
